32 devices in a mesh: sample: 2 (over x), row: 16 (over z, y, core).
Axes of the slice: x: 2, y: 2, z: 4, core: 2. Of those that a mesh axis runs over, the one named last changes fastest.
Arguments:
- atom_single: bfloat16 [16384, 128], P(('sample', 'row')), parts along dimension 0, may hold values from -6 to 6
- atom_count: int32 [16], replicated, may hold values from 128 to 512, as said below
- atom_token: int32 [8192], P('row'), may hold values from 0 to 63, as said below
- atom_bias: bfloat16 [256, 4, 32, 128], P('row'), may hold values from -4 to 236
- token_single: bfloat16 [2048, 768], P(('sample', 'row')), parts along dimension 0, may hold values from -6 to 6
- token_bias: bfloat16 [16, 1024, 1024], P(None, 'row'), may hold values from -4 to 236
- atom_gain: float32 [128], replicated, may hold values from 0.25 to 1.75
- atom_qkvg: bfloat16 [128, 512], replicated, may hold values from -0.5 to 0.5
- atom_proj: bfloat16 [128, 128], replicated, may hold values from -0.5 to 0.5
- atom_to_token: bfloat16 [128, 768], replicated, may hold values from -0.5 to 0.5
- token_gain: float32 [768], replicated, may hold values from 0.25 to 1.75
- token_qg: bfloat16 [768, 1536], replicated, may hold values from -0.21875 to 0.21875
- token_kv: bfloat16 [768, 1536], replicated, may hold values from -0.21875 to 0.21875
- token_proj: bfloat16 [768, 768], replicated, may hold values from -0.21875 to 0.21875
- token_to_atom: bfloat16 [768, 128], replicated, may hold values from -0.21875 to 0.21875
Outputs:
- atom_out: bfloat16 [16384, 128], P(('sample', 'row')), parts along dimension 0
- token_out: bfloat16 [2048, 768], P(('sample', 'row')), parts along dimension 0
The draws below stay inside these ranges and needn't reach their ends.
There are 2 independent parts, one for each index of `sample`. The reference program is written for one: setup_inputs(seed, part) draws one part's arguments, and reference() takes and returns one part's arrays. A program takes and returns all parts, laid end to end along the dimension named above; an argument that names none is the same for every part. Nothing has to cross between parts.
Inputs may be any that keep to these rules, and one draw needn't show every extreme that they name: `atom_count`: entry b counts the live slots of atoms b * 512 to (b + 1) * 512 - 1, which are the first ones of that block; some block has exactly 512 and another exactly 128. `atom_token`: within a block of 512 slots the live slots' values never fall and each of the 64 values occurs in at least one live slot; slots that are not live hold 0.
All inputs are finite; a program needn't handle non-finite values.
Results may differ from the reference program's by a relative error of at most 0.0051.
Values may be sent and summed in bfloat16 or wider, within the bound.
A program may use at most 128 MiB of HBM per device.

```python
import jax
import jax.numpy as jnp
from jax import lax

TW = 768
TH = 16
AW = 128
AH = 4
WQ = 32
WK = 128
TOK_DEV = 64
ATOM_DEV = 512
LEFT_RIM = 48
RIGHT_RIM = 80
N_TOK = 1024
ATOMS = 8192
BLOCKS = 256
N_ROW = 16


def layout(key):
    base = jax.random.fold_in(key, 101)
    streams = jax.random.split(base, 6)
    ligand = jax.random.randint(streams[0], (N_ROW,), 0, 4) == 0
    lowest = ATOM_DEV // 4
    heavy = jax.random.randint(streams[1], (N_ROW,), 5 * ATOM_DEV // 8, ATOM_DEV + 1)
    light = jax.random.randint(streams[2], (N_ROW,), lowest, 3 * ATOM_DEV // 8)
    counts = jnp.where(ligand, light, heavy)
    fullest = jax.random.randint(streams[3], (), 0, N_ROW)
    emptiest = (fullest + 1 + jax.random.randint(streams[4], (), 0, N_ROW - 1)) % N_ROW
    counts = counts.at[fullest].set(ATOM_DEV).at[emptiest].set(lowest)
    slots = jnp.arange(ATOM_DEV, dtype=jnp.int32)
    ranking = jax.random.randint(streams[5], (N_ROW, ATOM_DEV), 0, 2 ** 18)
    allowed = (slots[None, :] >= 1) & (slots[None, :] < counts[:, None])
    ranked = jnp.where(allowed, ranking * ATOM_DEV + slots[None, :], -1)
    chosen = lax.top_k(ranked, TOK_DEV - 1)[0]
    cuts = chosen % ATOM_DEV
    tokens = jnp.sum((cuts[:, None, :] <= slots[None, :, None]).astype(jnp.int32), axis=2)
    tokens = jnp.where(slots[None, :] < counts[:, None], tokens, 0)
    return (counts.astype(jnp.int32), tokens.reshape(N_ROW * ATOM_DEV).astype(jnp.int32))


def draw_atom_count(key, part):
    return layout(key)[0]


def draw_atom_token(key, part):
    return layout(key)[1]


def background(key, shape):
    return jnp.clip(jax.random.normal(key, shape, jnp.float32), -4.0, 4.0)


def draw_token_bias(key, part):
    streams = jax.random.split(jax.random.fold_in(key, 211), 1)
    values = background(streams[0], (TH, N_TOK, N_TOK))
    return values.astype(jnp.bfloat16)


def draw_atom_bias(key, part):
    streams = jax.random.split(jax.random.fold_in(key, 307), 1)
    values = background(streams[0], (BLOCKS, AH, WQ, WK))
    return values.astype(jnp.bfloat16)


def steps_of(stream_key, dims, pieces, low, top_value):
    level = 1.0
    for axis_at, blocks in pieces:
        heights = jax.random.uniform(jax.random.fold_in(jax.random.fold_in(stream_key, 6), axis_at), (blocks,), jnp.float32, low / len(pieces), top_value / len(pieces))
        level = level * jnp.repeat(jnp.exp(heights), dims[axis_at] // blocks).reshape((-1,) + (1,) * (len(dims) - 1 - axis_at))
    return level


def normal_values(stream_key, shape, scale, reach, shards=(), held_as=jnp.bfloat16):
    values = scale * jax.random.normal(stream_key, shape, jnp.float32)
    if shards:
        values = values * steps_of(stream_key, shape, shards, -0.22, 0.18)
    return jnp.clip(values, -reach, reach).astype(held_as)


def setup_inputs(seed: int = 0, part: int = 0) -> dict:
    key_of = jax.random.split(jax.random.key(seed), 16)
    part_splits = jax.random.split(jax.random.fold_in(key_of[15], part), 16)
    return {
        "atom_single": normal_values(part_splits[0], (ATOMS, AW), 1.0, 6.0, ((0, 16),)),
        "atom_count": draw_atom_count(jax.random.fold_in(key_of[15], 71), part),
        "atom_token": draw_atom_token(jax.random.fold_in(key_of[15], 71), part),
        "atom_bias": draw_atom_bias(jax.random.fold_in(key_of[15], 71), part),
        "token_single": normal_values(part_splits[4], (N_TOK, TW), 1.0, 6.0, ((0, 16),)),
        "token_bias": draw_token_bias(jax.random.fold_in(key_of[15], 71), part),
        "atom_gain": jnp.clip(1.0 + 0.15 * jax.random.normal(key_of[6], (AW,), jnp.float32), 0.25, 1.75),
        "atom_qkvg": normal_values(key_of[7], (AW, 4 * AW), AW ** -0.5, 0.5),
        "atom_proj": normal_values(key_of[8], (AW, AW), AW ** -0.5, 0.5),
        "atom_to_token": normal_values(key_of[9], (AW, TW), AW ** -0.5, 0.5),
        "token_gain": jnp.clip(1.0 + 0.15 * jax.random.normal(key_of[10], (TW,), jnp.float32), 0.25, 1.75),
        "token_qg": normal_values(key_of[11], (TW, 2 * TW), TW ** -0.5, 0.21875),
        "token_kv": normal_values(key_of[12], (TW, 2 * TW), TW ** -0.5, 0.21875),
        "token_proj": normal_values(key_of[13], (TW, TW), TW ** -0.5, 0.21875),
        "token_to_atom": normal_values(key_of[14], (TW, AW), TW ** -0.5, 0.21875),
    }


EPSILON = 1e-05
MASKED = -1000000000.0

def layer_norm(values, gain):
    floats = values.astype(jnp.float32)
    average = lax.optimization_barrier(jnp.mean(floats, axis=-1, keepdims=True))
    centred = floats - average
    spread = lax.optimization_barrier(jnp.mean(centred * centred, axis=-1, keepdims=True))
    return (centred * lax.rsqrt(spread + EPSILON) * gain).astype(jnp.bfloat16)

def window_attention(projected, before, after_rim, live_count, bias_block, is_first, is_last):
    blocks = ATOM_DEV // WQ
    head_size = AW // AH
    queries = projected[:, :AW].reshape(blocks, WQ, AH, head_size).astype(jnp.float32)
    keyval = projected[:, AW:3 * AW]
    extended = jnp.concatenate([before, keyval, jnp.zeros((RIGHT_RIM, 2 * AW), keyval.dtype)], axis=0)
    extended = lax.dynamic_update_slice_in_dim(extended, after_rim, (LEFT_RIM + live_count).astype(jnp.int32), 0)
    tile_rows = extended.reshape(blocks + WK // WQ, WQ, 2 * AW)
    windows = jnp.concatenate([tile_rows[offset_block:offset_block + blocks] for offset_block in range(WK // WQ)], axis=1)
    key_rows = windows[:, :, :AW].reshape(blocks, WK, AH, head_size).astype(jnp.float32)
    value_rows = windows[:, :, AW:].reshape(blocks, WK, AH, head_size).astype(jnp.float32)
    scores = jnp.einsum('bqhd,bkhd->bhqk', queries, key_rows) * head_size ** (-0.5) + bias_block.astype(jnp.float32)
    places = WQ * jnp.arange(blocks, dtype=jnp.int32)[:, None] - LEFT_RIM + jnp.arange(WK, dtype=jnp.int32)[None, :]
    usable = ((places >= 0) | jnp.logical_not(is_first)) & ((places < live_count) | jnp.logical_not(is_last))
    scores = jnp.where(usable[:, None, None, :], scores, MASKED)
    row_max = lax.optimization_barrier(jnp.max(scores, axis=-1, keepdims=True))
    raised = jnp.exp(scores - row_max)
    totals = lax.optimization_barrier(jnp.sum(raised, axis=-1))
    weights = raised.astype(jnp.bfloat16).astype(jnp.float32)
    attended = jnp.einsum('bhqk,bkhd->bqhd', weights, value_rows) / jnp.transpose(totals, (0, 2, 1))[:, :, :, None]
    return attended.reshape(ATOM_DEV, AW)

def reference(atom_single, atom_count, atom_token, atom_bias, token_single, token_bias, atom_gain, atom_qkvg, atom_proj, atom_to_token, token_gain, token_qg, token_kv, token_proj, token_to_atom):
    normed = layer_norm(atom_single, atom_gain)
    projected = jnp.dot(normed, atom_qkvg, preferred_element_type=jnp.float32).astype(jnp.bfloat16)
    projected = projected.reshape(N_ROW, ATOM_DEV, 4 * AW)
    keyval = projected[:, :, AW:3 * AW]
    tails = jax.vmap(lambda rows, number: lax.dynamic_slice_in_dim(rows, (number - LEFT_RIM).astype(jnp.int32), LEFT_RIM, 0))(keyval, atom_count)
    heads = keyval[:, :RIGHT_RIM]
    before = jnp.concatenate([jnp.zeros((1, LEFT_RIM, 2 * AW), keyval.dtype), tails[:-1]], axis=0)
    after_rim = jnp.concatenate([heads[1:], jnp.zeros((1, RIGHT_RIM, 2 * AW), keyval.dtype)], axis=0)
    bias_blocks = atom_bias.reshape(N_ROW, ATOM_DEV // WQ, AH, WQ, WK)
    devices = jnp.arange(N_ROW, dtype=jnp.int32)

    def per_device(items):
        rows, prior, later, number, bias_block, device_no = items
        return window_attention(rows, prior, later, number, bias_block, device_no == 0, device_no == N_ROW - 1)
    attended = lax.map(per_device, (projected, before, after_rim, atom_count, bias_blocks, devices))
    gate_part = projected[:, :, 3 * AW:].astype(jnp.float32)
    gated = (attended * jax.nn.sigmoid(gate_part)).astype(jnp.bfloat16).reshape(ATOMS, AW)
    atom_mid = (atom_single.astype(jnp.float32) + jnp.dot(gated, atom_proj, preferred_element_type=jnp.float32)).astype(jnp.bfloat16)
    offsets = jnp.arange(ATOM_DEV, dtype=jnp.int32)
    is_live = (offsets[None, :] < atom_count[:, None]).reshape(ATOMS)
    lifted = jax.nn.relu(jnp.dot(atom_mid, atom_to_token, preferred_element_type=jnp.float32)).astype(jnp.bfloat16)
    owner = (jnp.repeat(devices, ATOM_DEV) * TOK_DEV + atom_token).astype(jnp.int32)
    live_weight = is_live.astype(jnp.float32)
    summed = jax.ops.segment_sum(lifted.astype(jnp.float32) * live_weight[:, None], owner, num_segments=N_TOK)
    counts = jax.ops.segment_sum(live_weight, owner, num_segments=N_TOK)
    pooled = summed / counts[:, None]
    hidden = token_single.astype(jnp.float32) + pooled
    normed_tok = layer_norm(hidden, token_gain)
    query_gate = jnp.dot(normed_tok, token_qg, preferred_element_type=jnp.float32).astype(jnp.bfloat16)
    keyval_tok = jnp.dot(normed_tok, token_kv, preferred_element_type=jnp.float32).astype(jnp.bfloat16)
    head_size = TW // TH
    key_rows = keyval_tok[:, :TW].reshape(N_TOK, TH, head_size).astype(jnp.float32)
    value_rows = keyval_tok[:, TW:].reshape(N_TOK, TH, head_size).astype(jnp.float32)
    queries_all = query_gate[:, :TW].reshape(N_TOK, TH, head_size)

    def attend(device_no):
        queries = lax.dynamic_slice_in_dim(queries_all, device_no * TOK_DEV, TOK_DEV, 0).astype(jnp.float32)
        bias_tile = lax.dynamic_slice_in_dim(token_bias, device_no * TOK_DEV, TOK_DEV, 1).astype(jnp.float32)
        scores = jnp.einsum('qhd,khd->hqk', queries, key_rows) * head_size ** (-0.5) + bias_tile
        row_max = lax.optimization_barrier(jnp.max(scores, axis=-1, keepdims=True))
        raised = jnp.exp(scores - row_max)
        totals = lax.optimization_barrier(jnp.sum(raised, axis=-1))
        weights = raised.astype(jnp.bfloat16).astype(jnp.float32)
        result = jnp.einsum('hqk,khd->qhd', weights, value_rows) / jnp.transpose(totals)[:, :, None]
        return result.reshape(TOK_DEV, TW)
    attended_tok = lax.map(attend, devices).reshape(N_TOK, TW)
    gated_tok = (attended_tok * jax.nn.sigmoid(query_gate[:, TW:].astype(jnp.float32))).astype(jnp.bfloat16)
    token_out = (hidden + jnp.dot(gated_tok, token_proj, preferred_element_type=jnp.float32)).astype(jnp.bfloat16)
    lifted_back = jnp.dot(token_out, token_to_atom, preferred_element_type=jnp.float32)
    atom_out = jnp.where(is_live[:, None], atom_mid.astype(jnp.float32) + jnp.take(lifted_back, owner, axis=0), 0.0).astype(jnp.bfloat16)
    return (atom_out, token_out)
```

```python
import functools

import jax
import jax.numpy as jnp
from jax import lax
from jax.experimental import pallas as pl
from jax.experimental.pallas import tpu as pltpu
from jax.sharding import PartitionSpec as P

TH = 16
AH = 4
WQ = 32
WK = 128
LEFT_RIM = 48
RIGHT_RIM = 80
EPSILON = 1e-05
MASKED = -1000000000.0
PIECES = 2
F32 = jnp.float32
BF16 = jnp.bfloat16
MESH = pl.DeviceIdType.MESH


def normalized(values, gain):
    floats = values.astype(F32)
    average = jnp.mean(floats, axis=-1, keepdims=True)
    centred = floats - average
    spread = jnp.mean(centred * centred, axis=-1, keepdims=True)
    return (centred * lax.rsqrt(spread + EPSILON) * gain).astype(BF16)


def product(left, right):
    return jnp.dot(left, right, preferred_element_type=F32)


def product_t(left, right):
    return lax.dot_general(left, right, (((1,), (1,)), ((), ())), preferred_element_type=F32)


def iota(shape, dimension):
    return lax.broadcasted_iota(jnp.int32, shape, dimension)


def head_groups(heads, size):
    groups, head = [], 0
    while head < heads:
        base = head * size // 128 * 128
        base = min(base, heads * size - 256)
        last = head
        while last < heads and (last + 1) * size <= base + 256:
            last += 1
        groups.append((head, last, base))
        head = last
    return groups


def kernel(
    rows, ny,
    count_ref, x_hbm, again_hbm, qkvg_hbm, abias_hbm, token_hbm, tgain_hbm, aproj_hbm,
    a2t_hbm, tsingle_hbm, tqg_hbm, tkv_hbm, tbias_hbm, tproj_hbm, t2a_hbm,
    aout_ref, tout_ref,
    x_ref, again_ref, qkvg_ref, abias, token_ref, tgain_ref, aproj_ref,
    a2t, tsingle, tqg, tkv, tbias, tproj, t2a,
    rims, halo, ext, att, gathered, qbuf, mbuf, lbuf, acc,
    load_sem, halo_send, halo_recv, send_sem, recv_sem,
):
    atoms, aw = x_ref.shape
    toks, tw = tsingle.shape
    ahead = aw // AH
    thead = tw // TH
    me = lax.axis_index("row")
    core = me % 2
    chip = me // 2
    y = chip % ny
    z = chip // ny
    nz = rows // (2 * ny)
    groups = head_groups(TH, thead)

    def index(zz, yy, cc):
        return (zz * ny + yy) * 2 + cc

    sibling = index(z, y, 1 - core)
    other = index(z, 1 - y, core)
    up = index(z + 1, y, core)
    down = index(z - 1, y, core)

    barrier = pltpu.get_barrier_semaphore()

    def greet(target):
        pl.semaphore_signal(barrier, inc=1, device_id={"row": target}, device_id_type=MESH)

    greet(sibling)
    if ny > 1:
        greet(other)
    pl.when(z + 1 < nz)(lambda: greet(up))
    pl.when(z > 0)(lambda: greet(down))
    pl.when(me + 1 < rows)(lambda: greet(me + 1))
    pl.when(me > 0)(lambda: greet(me - 1))

    loads = [
        pltpu.make_async_copy(source, target, load_sem.at[place])
        for place, (source, target) in enumerate(
            (
                (x_hbm, x_ref), (again_hbm, again_ref), (qkvg_hbm, qkvg_ref), (abias_hbm, abias),
                (token_hbm, token_ref), (tgain_hbm, tgain_ref), (aproj_hbm, aproj_ref), (a2t_hbm, a2t),
                (tsingle_hbm, tsingle), (tqg_hbm, tqg), (tkv_hbm, tkv), (tbias_hbm, tbias),
                (tproj_hbm, tproj), (t2a_hbm, t2a),
            )
        )
    ]
    for load in loads:
        load.start()
    (
        load_x, load_again, load_qkvg, load_abias, load_token, load_tgain, load_aproj, load_a2t,
        load_tsingle, load_tqg, load_tkv, load_tbias, load_tproj, load_t2a,
    ) = loads

    count = count_ref[me]

    @pl.when(me == 0)
    def _():
        halo[0:LEFT_RIM, :] = jnp.zeros((LEFT_RIM, 2 * aw), BF16)

    @pl.when(me == rows - 1)
    def _():
        halo[LEFT_RIM:, :] = jnp.zeros((RIGHT_RIM, 2 * aw), BF16)

    load_x.wait()
    load_again.wait()
    load_qkvg.wait()
    x = x_ref[...]
    projected = product(normalized(x, again_ref[...]), qkvg_ref[...]).astype(BF16)
    queries = projected[:, :aw]
    gates = jax.nn.sigmoid(projected[:, 3 * aw :].astype(F32))
    keyval = projected[:, aw : 3 * aw]
    pick = (iota((LEFT_RIM, atoms), 1) == iota((LEFT_RIM, atoms), 0) + (count - LEFT_RIM))
    rims[0:LEFT_RIM, :] = product(pick.astype(F32).astype(BF16), keyval).astype(BF16)
    rims[LEFT_RIM:, :] = keyval[:RIGHT_RIM]

    pl.semaphore_wait(
        barrier,
        1 + (1 if ny > 1 else 0)
        + jnp.where(z + 1 < nz, 1, 0) + jnp.where(z > 0, 1, 0)
        + jnp.where(me + 1 < rows, 1, 0) + jnp.where(me > 0, 1, 0),
    )

    to_next = pltpu.make_async_remote_copy(
        rims.at[pl.ds(0, LEFT_RIM)], halo.at[pl.ds(0, LEFT_RIM)], halo_send.at[0], halo_recv.at[0],
        device_id={"row": me + 1}, device_id_type=MESH,
    )
    to_prior = pltpu.make_async_remote_copy(
        rims.at[pl.ds(LEFT_RIM, RIGHT_RIM)], halo.at[pl.ds(LEFT_RIM, RIGHT_RIM)],
        halo_send.at[1], halo_recv.at[1],
        device_id={"row": me - 1}, device_id_type=MESH,
    )
    pl.when(me + 1 < rows)(to_next.start)
    pl.when(me > 0)(to_prior.start)

    blocks = atoms // WQ
    lane_head = iota((AH * WQ, aw), 1) // ahead
    own_head = (lane_head == iota((AH * WQ, aw), 0) // WQ).astype(F32)
    own_head_half = own_head.astype(BF16)
    span = atoms + RIGHT_RIM
    place = iota((span, WK), 0) - count
    chosen = ((place == iota((span, WK), 1) - LEFT_RIM) & (place >= 0)).astype(F32).astype(BF16)
    within = iota((span, 2 * aw), 0) - count
    within = (within >= 0) & (within < RIGHT_RIM)
    base_rows = jnp.concatenate(
        [keyval.astype(F32), jnp.zeros((RIGHT_RIM, 2 * aw), F32)], axis=0
    )
    load_abias.wait()
    load_token.wait()
    load_tgain.wait()
    load_aproj.wait()
    load_a2t.wait()
    load_tsingle.wait()
    pl.when(me > 0)(to_next.wait_recv)
    pl.when(me + 1 < rows)(to_prior.wait_recv)
    rim = halo[...]
    moved = product(chosen, rim)
    ext[0:LEFT_RIM, :] = rim[:LEFT_RIM]
    ext[LEFT_RIM:, :] = jnp.where(within, moved, base_rows).astype(BF16)

    is_first = me == 0
    is_last = me == rows - 1
    low = jnp.where(is_first, 0, -LEFT_RIM)
    high = jnp.where(is_last, count, atoms + WK)
    for start_at in range(0, blocks, 8):
        batch = range(start_at, min(start_at + 8, blocks))
        scores = []
        for w in batch:
            q = queries[w * WQ : (w + 1) * WQ]
            stacked = jnp.concatenate([q] * AH, axis=0) * own_head_half
            scores.append(product_t(stacked, ext[w * WQ : w * WQ + WK, :aw]))
        for at, w in enumerate(batch):
            value = scores[at] * ahead ** (-0.5) + abias[w].reshape(AH * WQ, WK).astype(F32)
            offset = iota((AH * WQ, WK), 1) + (WQ * w - LEFT_RIM)
            scores[at] = jnp.where((offset >= low) & (offset < high), value, MASKED)
        tops = [jnp.max(value, axis=-1, keepdims=True) for value in scores]
        raised = [jnp.exp(value - top) for value, top in zip(scores, tops)]
        totals = [jnp.sum(value, axis=-1, keepdims=True) for value in raised]
        results = [
            product(raised[at].astype(BF16), ext[w * WQ : w * WQ + WK, aw:])
            for at, w in enumerate(batch)
        ]
        for at, w in enumerate(batch):
            result = results[at] * own_head / totals[at]
            att[w * WQ : (w + 1) * WQ, :] = jnp.sum(result.reshape(AH, WQ, aw), axis=0)
    gated = (att[...] * gates).astype(BF16)
    atom_mid = (x.astype(F32) + product(gated, aproj_ref[...])).astype(BF16)
    lifted = jnp.maximum(product(atom_mid, a2t[...]), 0.0).astype(BF16)
    member = (token_ref[...] == iota((toks, atoms), 0)) & (iota((toks, atoms), 1) < count)
    member_f = member.astype(F32)
    summed = product(member_f.astype(BF16), lifted)
    counts = jnp.sum(member_f, axis=1, keepdims=True)
    hidden = tsingle[...].astype(F32) + summed / counts
    normed = normalized(hidden, tgain_ref[...].reshape(1, tw))
    gathered[me] = normed

    piece_rows = toks // PIECES

    def copy(source, piece, way, target):
        view = gathered.at[source, pl.ds(piece * piece_rows, piece_rows)]
        return pltpu.make_async_remote_copy(
            view, view, send_sem.at[source, piece, way], recv_sem.at[source, piece],
            device_id={"row": target}, device_id_type=MESH,
        )

    def pass_up(source, piece, act):
        pl.when(z + 1 < nz)(lambda: act(copy(source, piece, 2, up)))

    def pass_down(source, piece, act):
        pl.when(z > 0)(lambda: act(copy(source, piece, 3, down)))

    def pass_near(source, piece, act):
        if ny > 1:
            act(copy(source, piece, 1, other))
        act(copy(source, piece, 0, sibling))

    start = lambda c: c.start()
    sent = lambda c: c.wait_send()

    def arrived(source, piece):
        copy(source, piece, 0, sibling).wait_recv()

    def own(act):
        for piece in range(PIECES):
            pass_up(me, piece, act)
            pass_down(me, piece, act)
            pass_near(me, piece, act)

    def along_z(distance, act, wait):
        for piece in range(PIECES):
            @pl.when(z - distance >= 0)
            def _():
                source = index(z - distance, y, core)
                if wait:
                    arrived(source, piece)
                pass_up(source, piece, act)
                pass_near(source, piece, act)

            @pl.when(z + distance < nz)
            def _():
                source = index(z + distance, y, core)
                if wait:
                    arrived(source, piece)
                pass_down(source, piece, act)
                pass_near(source, piece, act)

    def along_y(distance, act, wait):
        if ny == 1:
            return
        for piece in range(PIECES):
            for sign in (-1, 1):
                zz = z + sign * distance

                @pl.when((zz >= 0) & (zz < nz) & ((sign < 0) | (distance > 0)))
                def _():
                    source = index(zz, 1 - y, core)
                    if wait:
                        arrived(source, piece)
                    act(copy(source, piece, 0, sibling))

    own(start)
    turned = member_f.T.astype(BF16)

    load_tqg.wait()
    qgate = product(normed, tqg[...]).astype(BF16)
    tok_gate = jax.nn.sigmoid(qgate[:, tw:].astype(F32))
    row = 0
    for first, last, base in groups:
        part = qgate[:, base : base + 256].astype(F32)
        lanes = iota(part.shape, 1) + base
        for head in range(first, last):
            keep = (lanes >= head * thead) & (lanes < (head + 1) * thead)
            qbuf[row : row + toks, :] = jnp.where(keep, part, 0.0).astype(BF16)
            row += toks
    mbuf[...] = jnp.full(mbuf.shape, -jnp.inf, F32)
    lbuf[...] = jnp.zeros(lbuf.shape, F32)
    acc[...] = jnp.zeros(acc.shape, F32)
    load_tkv.wait()
    load_tbias.wait()

    def attend(block):
        inputs = gathered[pl.ds(2 * block, 2)].reshape(2 * toks, tw)
        kv = product(inputs, tkv[...]).astype(BF16)
        columns = pl.ds(pl.multiple_of(block * 2 * toks, 2 * toks), 2 * toks)
        for first, last, base in groups:
            part = slice(first * toks, last * toks)
            bias = tbias[first:last, :, columns].reshape((last - first) * toks, 2 * toks)
            scores = product_t(qbuf[part, :], kv[:, base : base + 256])
            scores = scores * thead ** (-0.5) + bias.astype(F32)
            old = mbuf[part, :]
            new = jnp.maximum(old, jnp.max(scores, axis=-1, keepdims=True))
            factor = jnp.exp(old - new)
            raised = jnp.exp(scores - new)
            mbuf[part, :] = new
            lbuf[part, :] = lbuf[part, :] * factor + raised
            update = product(raised.astype(BF16), kv[:, tw + base : tw + base + 256])
            for half in (slice(0, 128), slice(128, 256)):
                acc[part, half] = acc[part, half] * factor + update[:, half]

    def step(t, carry):
        distance = t // (2 * ny)
        turn = t % (2 * ny)

        @pl.when(turn == 0)
        def _():
            along_z(distance + 1, start, True)

        @pl.when(turn == 1)
        def _():
            along_y(distance, start, True)

        yy = jnp.where(turn // 2 == 0, y, 1 - y)
        sign = turn % 2
        zz = z + (2 * sign - 1) * distance

        @pl.when((zz >= 0) & (zz < nz) & ((sign == 0) | (distance > 0)))
        def _():
            for piece in range(PIECES):
                arrived(index(zz, yy, 1 - core), piece)
            attend(zz * ny + yy)

        return carry

    lax.fori_loop(0, nz * 2 * ny, step, 0)

    pieces = [None] * (tw // 128)
    for first, last, base in groups:
        lanes = iota((toks, 256), 1) + base
        total = jnp.zeros((toks, 256), F32)
        for head in range(first, last):
            part = slice(head * toks, (head + 1) * toks)
            whole = jnp.sum(lbuf[part, :], axis=-1, keepdims=True)
            keep = (lanes >= head * thead) & (lanes < (head + 1) * thead)
            total = total + jnp.where(keep, acc[part, :] / whole, 0.0)
        for half in (0, 1):
            at = base // 128 + half
            value = total[:, half * 128 : (half + 1) * 128]
            pieces[at] = value if pieces[at] is None else pieces[at] + value
    attended = jnp.concatenate(pieces, axis=1)
    tok_gated = (attended * tok_gate).astype(BF16)
    load_tproj.wait()
    token_out = (hidden + product(tok_gated, tproj[...])).astype(BF16)
    tout_ref[...] = token_out
    load_t2a.wait()
    back = product(token_out, t2a[...])
    high_part = back.astype(BF16)
    rest = back - high_part.astype(F32)
    mid_part = rest.astype(BF16)
    low_part = (rest - mid_part.astype(F32)).astype(BF16)
    spread = product(turned, high_part) + product(turned, mid_part) + product(turned, low_part)
    live = iota((atoms, aw), 0) < count
    aout_ref[...] = jnp.where(live, atom_mid.astype(F32) + spread, 0.0).astype(BF16)

    pl.when(me + 1 < rows)(to_next.wait_send)
    pl.when(me > 0)(to_prior.wait_send)
    own(sent)

    def drain(distance, carry):
        along_z(distance, sent, False)
        along_y(distance - 1, sent, False)
        return carry

    lax.fori_loop(1, nz, drain, 0)
    along_y(nz - 1, sent, False)


def hand_on(a_ref, t_ref, aout_ref, tout_ref, sem):
    copies = [
        pltpu.make_async_copy(a_ref, aout_ref, sem.at[0]),
        pltpu.make_async_copy(t_ref, tout_ref, sem.at[1]),
    ]
    for copy in copies:
        copy.start()
    for copy in copies:
        copy.wait()


def on_device(
    rows, ny, atom_single, atom_count, atom_token, atom_bias, token_single, token_bias,
    atom_gain, atom_qkvg, atom_proj, atom_to_token, token_gain, token_qg, token_kv,
    token_proj, token_to_atom,
):
    atoms, aw = atom_single.shape
    toks, tw = token_single.shape
    vmem = pl.BlockSpec(memory_space=pltpu.VMEM)
    anywhere = pl.BlockSpec(memory_space=pl.ANY)
    taken = [
        atom_single, atom_gain.reshape(1, aw), atom_qkvg, atom_bias, atom_token.reshape(1, atoms), token_gain,
        atom_proj, atom_to_token, token_single, token_qg, token_kv, token_bias, token_proj, token_to_atom,
    ]
    results = pl.pallas_call(
        functools.partial(kernel, rows, ny),
        out_shape=(pltpu.VMEM((atoms, aw), BF16), pltpu.VMEM((toks, tw), BF16)),
        in_specs=[pl.BlockSpec(memory_space=pltpu.SMEM)] + [anywhere] * len(taken),
        out_specs=(vmem, vmem),
        scratch_shapes=[pltpu.VMEM(a.shape, a.dtype) for a in taken]
        + [
            pltpu.VMEM((LEFT_RIM + RIGHT_RIM, 2 * aw), BF16),
            pltpu.VMEM((LEFT_RIM + RIGHT_RIM, 2 * aw), BF16),
            pltpu.VMEM((LEFT_RIM + atoms + RIGHT_RIM, 2 * aw), BF16),
            pltpu.VMEM((atoms, aw), F32),
            pltpu.VMEM((rows, toks, tw), BF16),
            pltpu.VMEM((TH * toks, 256), BF16),
            pltpu.VMEM((TH * toks, 128), F32),
            pltpu.VMEM((TH * toks, 128), F32),
            pltpu.VMEM((TH * toks, 256), F32),
            pltpu.SemaphoreType.DMA((len(taken),)),
            pltpu.SemaphoreType.DMA((2,)),
            pltpu.SemaphoreType.DMA((2,)),
            pltpu.SemaphoreType.DMA((rows, PIECES, 4)),
            pltpu.SemaphoreType.DMA((rows, PIECES)),
        ],
        compiler_params=pltpu.CompilerParams(collective_id=0, has_side_effects=True),
    )(atom_count, *taken)
    held = [pltpu.with_memory_space_constraint(r, pltpu.VMEM) for r in results]
    return pl.pallas_call(
        hand_on,
        out_shape=tuple(jax.ShapeDtypeStruct(r.shape, r.dtype) for r in results),
        in_specs=(vmem, vmem),
        out_specs=(anywhere, anywhere),
        scratch_shapes=[pltpu.SemaphoreType.DMA((2,))],
    )(*held)


def chips_across(mesh):
    rows = mesh.shape["row"]
    group = mesh.devices.reshape(-1)[:rows]
    places = [getattr(device, "coords", None) for device in group]
    if any(place is None for place in places):
        return 1
    wide = len({place[1] for place in places})
    return 2 if wide == 2 and rows % 4 == 0 else 1


def solution(mesh):
    rows = mesh.shape["row"]
    return jax.shard_map(
        functools.partial(on_device, rows, chips_across(mesh)),
        mesh=mesh,
        in_specs=(
            P(("sample", "row"), None),
            P(),
            P("row"),
            P("row", None, None, None),
            P(("sample", "row"), None),
            P(None, "row", None),
            P(), P(), P(), P(), P(), P(), P(), P(), P(),
        ),
        out_specs=(P(("sample", "row"), None), P(("sample", "row"), None)),
        check_vma=False,
    )
```

```python
import functools

import jax
import jax.numpy as jnp
from jax import lax
from jax.experimental import pallas as pl
from jax.experimental.pallas import tpu as pltpu
from jax.sharding import PartitionSpec as P

TH = 16
AH = 4
WQ = 32
WK = 128
LEFT_RIM = 48
RIGHT_RIM = 80
EPSILON = 1e-05
MASKED = -1000000000.0
PIECES = 2
EACH = 4
F32 = jnp.float32
BF16 = jnp.bfloat16
MESH = pl.DeviceIdType.MESH


def normalized(values, gain):
    floats = values.astype(F32)
    average = jnp.mean(floats, axis=-1, keepdims=True)
    centred = floats - average
    spread = jnp.mean(centred * centred, axis=-1, keepdims=True)
    return (centred * lax.rsqrt(spread + EPSILON) * gain).astype(BF16)


def product(left, right):
    return jnp.dot(left, right, preferred_element_type=F32)


def product_t(left, right):
    return lax.dot_general(left, right, (((1,), (1,)), ((), ())), preferred_element_type=F32)


def iota(shape, dimension):
    return lax.broadcasted_iota(jnp.int32, shape, dimension)


def head_groups(heads, size, each):
    return [(first, min(first * size // 128 * 128, heads * size - 256)) for first in range(0, heads, each)]


def kernel(
    rows, ny,
    count_ref, x_hbm, again_hbm, qkvg_hbm, abias_hbm, token_hbm, tgain_hbm, aproj_hbm,
    a2t_hbm, tsingle_hbm, tqg_hbm, tkv_hbm, tbias_hbm, tproj_hbm, t2a_hbm,
    aout_ref, tout_ref,
    x_ref, again_ref, qkvg_ref, abias, token_ref, tgain_ref, aproj_ref,
    a2t, tsingle, tqg, tkv, tbias, tproj, t2a,
    rims, halo, ext, att, gathered, qbuf, turned_bias, turned_gate, mbuf, lbuf, acc,
    load_sem, halo_send, halo_recv, send_sem, recv_sem,
):
    atoms, aw = x_ref.shape
    toks, tw = tsingle.shape
    ahead = aw // AH
    thead = tw // TH
    me = lax.axis_index("row")
    core = me % 2
    chip = me // 2
    y = chip % ny
    z = chip // ny
    nz = rows // (2 * ny)
    groups = head_groups(TH, thead, EACH)
    wide = EACH * toks

    def index(zz, yy, cc):
        return (zz * ny + yy) * 2 + cc

    sibling = index(z, y, 1 - core)
    other = index(z, 1 - y, core)
    up = index(z + 1, y, core)
    down = index(z - 1, y, core)

    barrier = pltpu.get_barrier_semaphore()

    def greet(target):
        pl.semaphore_signal(barrier, inc=1, device_id={"row": target}, device_id_type=MESH)

    greet(sibling)
    if ny > 1:
        greet(other)
    pl.when(z + 1 < nz)(lambda: greet(up))
    pl.when(z > 0)(lambda: greet(down))
    pl.when(me + 1 < rows)(lambda: greet(me + 1))
    pl.when(me > 0)(lambda: greet(me - 1))

    loads = [
        pltpu.make_async_copy(source, target, load_sem.at[place])
        for place, (source, target) in enumerate(
            (
                (x_hbm, x_ref), (again_hbm, again_ref), (qkvg_hbm, qkvg_ref), (abias_hbm, abias),
                (token_hbm, token_ref), (tgain_hbm, tgain_ref), (aproj_hbm, aproj_ref), (a2t_hbm, a2t),
                (tsingle_hbm, tsingle), (tqg_hbm, tqg), (tkv_hbm, tkv), (tbias_hbm, tbias),
                (tproj_hbm, tproj), (t2a_hbm, t2a),
            )
        )
    ]
    for load in loads:
        load.start()
    (
        load_x, load_again, load_qkvg, load_abias, load_token, load_tgain, load_aproj, load_a2t,
        load_tsingle, load_tqg, load_tkv, load_tbias, load_tproj, load_t2a,
    ) = loads

    count = count_ref[me]

    @pl.when(me == 0)
    def _():
        halo[0:LEFT_RIM, :] = jnp.zeros((LEFT_RIM, 2 * aw), BF16)

    @pl.when(me == rows - 1)
    def _():
        halo[LEFT_RIM:, :] = jnp.zeros((RIGHT_RIM, 2 * aw), BF16)

    load_x.wait()
    load_again.wait()
    load_qkvg.wait()
    x = x_ref[...]
    projected = product(normalized(x, again_ref[...]), qkvg_ref[...]).astype(BF16)
    queries = projected[:, :aw]
    gates = jax.nn.sigmoid(projected[:, 3 * aw :].astype(F32))
    keyval = projected[:, aw : 3 * aw]
    pick = (iota((LEFT_RIM, atoms), 1) == iota((LEFT_RIM, atoms), 0) + (count - LEFT_RIM))
    rims[0:LEFT_RIM, :] = product(pick.astype(F32).astype(BF16), keyval).astype(BF16)
    rims[LEFT_RIM:, :] = keyval[:RIGHT_RIM]

    pl.semaphore_wait(
        barrier,
        1 + (1 if ny > 1 else 0)
        + jnp.where(z + 1 < nz, 1, 0) + jnp.where(z > 0, 1, 0)
        + jnp.where(me + 1 < rows, 1, 0) + jnp.where(me > 0, 1, 0),
    )

    to_next = pltpu.make_async_remote_copy(
        rims.at[pl.ds(0, LEFT_RIM)], halo.at[pl.ds(0, LEFT_RIM)], halo_send.at[0], halo_recv.at[0],
        device_id={"row": me + 1}, device_id_type=MESH,
    )
    to_prior = pltpu.make_async_remote_copy(
        rims.at[pl.ds(LEFT_RIM, RIGHT_RIM)], halo.at[pl.ds(LEFT_RIM, RIGHT_RIM)],
        halo_send.at[1], halo_recv.at[1],
        device_id={"row": me - 1}, device_id_type=MESH,
    )
    pl.when(me + 1 < rows)(to_next.start)
    pl.when(me > 0)(to_prior.start)

    blocks = atoms // WQ
    lane_head = iota((AH * WQ, aw), 1) // ahead
    own_head = (lane_head == iota((AH * WQ, aw), 0) // WQ).astype(F32)
    own_head_half = own_head.astype(BF16)
    span = atoms + RIGHT_RIM
    place = iota((span, WK), 0) - count
    chosen = ((place == iota((span, WK), 1) - LEFT_RIM) & (place >= 0)).astype(F32).astype(BF16)
    within = iota((span, 2 * aw), 0) - count
    within = (within >= 0) & (within < RIGHT_RIM)
    base_rows = jnp.concatenate(
        [keyval.astype(F32), jnp.zeros((RIGHT_RIM, 2 * aw), F32)], axis=0
    )
    ext[:, 2 * aw :] = jnp.ones((ext.shape[0], aw), BF16)
    load_abias.wait()
    load_token.wait()
    load_tgain.wait()
    load_aproj.wait()
    load_a2t.wait()
    load_tsingle.wait()
    pl.when(me > 0)(to_next.wait_recv)
    pl.when(me + 1 < rows)(to_prior.wait_recv)
    rim = halo[...]
    moved = product(chosen, rim)
    ext[0:LEFT_RIM, : 2 * aw] = rim[:LEFT_RIM]
    ext[LEFT_RIM:, : 2 * aw] = jnp.where(within, moved, base_rows).astype(BF16)

    is_first = me == 0
    is_last = me == rows - 1
    low = jnp.where(is_first, 0, -LEFT_RIM)
    high = jnp.where(is_last, count, atoms + WK)
    for start_at in range(0, blocks, 8):
        batch = range(start_at, min(start_at + 8, blocks))
        scores = []
        for w in batch:
            q = queries[w * WQ : (w + 1) * WQ]
            stacked = jnp.concatenate([q] * AH, axis=0) * own_head_half
            scores.append(product_t(stacked, ext[w * WQ : w * WQ + WK, :aw]))
        for at, w in enumerate(batch):
            value = scores[at] * ahead ** (-0.5) + abias[w].reshape(AH * WQ, WK).astype(F32)
            offset = iota((AH * WQ, WK), 1) + (WQ * w - LEFT_RIM)
            scores[at] = jnp.where((offset >= low) & (offset < high), value, MASKED)
        tops = [jnp.max(value, axis=-1, keepdims=True) for value in scores]
        raised = [jnp.exp(value - top) for value, top in zip(scores, tops)]
        results = [
            product(raised[at].astype(BF16), ext[w * WQ : w * WQ + WK, aw:])
            for at, w in enumerate(batch)
        ]
        for at, w in enumerate(batch):
            result = results[at][:, :aw] * own_head / results[at][:, aw:]
            att[w * WQ : (w + 1) * WQ, :] = jnp.sum(result.reshape(AH, WQ, aw), axis=0)
    gated = (att[...] * gates).astype(BF16)
    atom_mid = (x.astype(F32) + product(gated, aproj_ref[...])).astype(BF16)
    lifted = jnp.maximum(product(atom_mid, a2t[...]), 0.0).astype(BF16)
    member = (token_ref[...] == iota((toks, atoms), 0)) & (iota((toks, atoms), 1) < count)
    member_f = member.astype(F32)
    summed = product(member_f.astype(BF16), lifted)
    counts = jnp.sum(member_f, axis=1, keepdims=True)
    hidden = tsingle[...].astype(F32) + summed / counts
    normed = normalized(hidden, tgain_ref[...].reshape(1, tw))
    gathered[me] = normed

    piece_rows = toks // PIECES

    def copy(source, piece, way, target):
        view = gathered.at[source, pl.ds(piece * piece_rows, piece_rows)]
        return pltpu.make_async_remote_copy(
            view, view, send_sem.at[source, piece, way], recv_sem.at[source, piece],
            device_id={"row": target}, device_id_type=MESH,
        )

    def pass_up(source, piece, act):
        pl.when(z + 1 < nz)(lambda: act(copy(source, piece, 2, up)))

    def pass_down(source, piece, act):
        pl.when(z > 0)(lambda: act(copy(source, piece, 3, down)))

    def pass_near(source, piece, act):
        if ny > 1:
            act(copy(source, piece, 1, other))
        act(copy(source, piece, 0, sibling))

    start = lambda c: c.start()
    sent = lambda c: c.wait_send()

    def arrived(source, piece):
        copy(source, piece, 0, sibling).wait_recv()

    def own(act):
        for piece in range(PIECES):
            pass_up(me, piece, act)
            pass_down(me, piece, act)
            pass_near(me, piece, act)

    def along_z(distance, act, wait):
        for piece in range(PIECES):
            @pl.when(z - distance >= 0)
            def _():
                source = index(z - distance, y, core)
                if wait:
                    arrived(source, piece)
                pass_up(source, piece, act)
                pass_near(source, piece, act)

            @pl.when(z + distance < nz)
            def _():
                source = index(z + distance, y, core)
                if wait:
                    arrived(source, piece)
                pass_down(source, piece, act)
                pass_near(source, piece, act)

    def along_y(distance, act, wait):
        if ny == 1:
            return
        for piece in range(PIECES):
            for sign in (-1, 1):
                zz = z + sign * distance

                @pl.when((zz >= 0) & (zz < nz) & ((sign < 0) | (distance > 0)))
                def _():
                    source = index(zz, 1 - y, core)
                    if wait:
                        arrived(source, piece)
                    act(copy(source, piece, 0, sibling))

    own(start)
    turned = jnp.concatenate([member_f, member_f], axis=0).T.astype(BF16)

    load_tqg.wait()
    qgate = product(normed, tqg[...]).astype(BF16)
    turned_gate[...] = jax.nn.sigmoid(qgate[:, tw:].T.astype(F32))
    for group, (first, base) in enumerate(groups):
        part = qgate[:, base : base + 256].astype(F32)
        lanes = iota(part.shape, 1) + base
        spread_out = []
        for head in range(first, first + EACH):
            keep = (lanes >= head * thead) & (lanes < (head + 1) * thead)
            spread_out.append(jnp.where(keep, part, 0.0).astype(BF16))
        qbuf[group] = jnp.concatenate(spread_out, axis=0).T
    mbuf[...] = jnp.full(mbuf.shape, -jnp.inf, F32)
    lbuf[...] = jnp.zeros(lbuf.shape, F32)
    acc[...] = jnp.zeros(acc.shape, F32)
    load_tkv.wait()
    load_tbias.wait()

    def turn_bias(block, carry):
        keys = pl.ds(pl.multiple_of(block * 2 * toks, 2 * toks), 2 * toks)
        turned_bias[keys, :] = tbias[:, :, keys].reshape(TH * toks, 2 * toks).T
        return carry

    lax.fori_loop(0, rows // 2, turn_bias, 0)
    low_half = iota((thead, wide // 2), 1) < toks

    def attend(block):
        inputs = gathered[pl.ds(2 * block, 2)].reshape(2 * toks, tw)
        kv = product(inputs, tkv[...]).astype(BF16)
        turned_values = kv[:, tw:].T
        keys = pl.ds(pl.multiple_of(block * 2 * toks, 2 * toks), 2 * toks)
        scores = jnp.concatenate(
            [product(kv[:, base : base + 256], qbuf[group]) for group, (first, base) in enumerate(groups)], axis=1
        )
        scores = scores * thead ** (-0.5) + turned_bias[keys, :].astype(F32)
        old = mbuf[...]
        new = jnp.maximum(old, jnp.max(scores, axis=0, keepdims=True))
        factor = jnp.exp(old - new)
        raised = jnp.exp(scores - new)
        mbuf[...] = new
        lbuf[...] = lbuf[...] * factor + jnp.sum(raised, axis=0, keepdims=True)
        weights = raised.astype(BF16)
        updates = [
            product(turned_values[first * thead : (first + EACH) * thead], weights[:, group * wide : (group + 1) * wide])
            for group, (first, base) in enumerate(groups)
        ]
        both = []
        for update in updates:
            for half in range(EACH // 2):
                lanes = slice(half * 2 * toks, (half + 1) * 2 * toks)
                top = 2 * half * thead
                both.append(jnp.where(low_half, update[top : top + thead, lanes], update[top + thead : top + 2 * thead, lanes]))
        acc[...] = acc[...] * factor + jnp.concatenate(both, axis=1)

    def step(t, carry):
        distance = t // (2 * ny)
        turn = t % (2 * ny)

        @pl.when(turn == 0)
        def _():
            along_z(distance + 1, start, True)

        @pl.when(turn == 1)
        def _():
            along_y(distance, start, True)

        yy = jnp.where(turn // 2 == 0, y, 1 - y)
        sign = turn % 2
        zz = z + (2 * sign - 1) * distance

        @pl.when((zz >= 0) & (zz < nz) & ((sign == 0) | (distance > 0)))
        def _():
            for piece in range(PIECES):
                arrived(index(zz, yy, 1 - core), piece)
            attend(zz * ny + yy)

        return carry

    lax.fori_loop(0, nz * 2 * ny, step, 0)

    whole = acc[...] / lbuf[...]
    columns = [whole[:, head * toks : (head + 1) * toks] for head in range(TH)]
    attended = jnp.concatenate(columns, axis=0)
    tok_gated = (attended * turned_gate[...]).astype(BF16).T
    load_tproj.wait()
    token_out = (hidden + product(tok_gated, tproj[...])).astype(BF16)
    tout_ref[...] = token_out
    load_t2a.wait()
    back = product(token_out, t2a[...])
    high_part = back.astype(BF16)
    rest = back - high_part.astype(F32)
    spread = product(turned, jnp.concatenate([high_part, rest.astype(BF16)], axis=0))
    live = iota((atoms, aw), 0) < count
    aout_ref[...] = jnp.where(live, atom_mid.astype(F32) + spread, 0.0).astype(BF16)

    pl.when(me + 1 < rows)(to_next.wait_send)
    pl.when(me > 0)(to_prior.wait_send)
    own(sent)

    def drain(distance, carry):
        along_z(distance, sent, False)
        along_y(distance - 1, sent, False)
        return carry

    lax.fori_loop(1, nz, drain, 0)
    along_y(nz - 1, sent, False)


def hand_on(a_ref, t_ref, aout_ref, tout_ref, sem):
    copies = [
        pltpu.make_async_copy(a_ref, aout_ref, sem.at[0]),
        pltpu.make_async_copy(t_ref, tout_ref, sem.at[1]),
    ]
    for copy in copies:
        copy.start()
    for copy in copies:
        copy.wait()


def on_device(
    rows, ny, atom_single, atom_count, atom_token, atom_bias, token_single, token_bias,
    atom_gain, atom_qkvg, atom_proj, atom_to_token, token_gain, token_qg, token_kv,
    token_proj, token_to_atom,
):
    atoms, aw = atom_single.shape
    toks, tw = token_single.shape
    vmem = pl.BlockSpec(memory_space=pltpu.VMEM)
    anywhere = pl.BlockSpec(memory_space=pl.ANY)
    taken = [
        atom_single, atom_gain.reshape(1, aw), atom_qkvg, atom_bias, atom_token.reshape(1, atoms), token_gain,
        atom_proj, atom_to_token, token_single, token_qg, token_kv, token_bias, token_proj, token_to_atom,
    ]
    results = pl.pallas_call(
        functools.partial(kernel, rows, ny),
        out_shape=(pltpu.VMEM((atoms, aw), BF16), pltpu.VMEM((toks, tw), BF16)),
        in_specs=[pl.BlockSpec(memory_space=pltpu.SMEM)] + [anywhere] * len(taken),
        out_specs=(vmem, vmem),
        scratch_shapes=[pltpu.VMEM(a.shape, a.dtype) for a in taken]
        + [
            pltpu.VMEM((LEFT_RIM + RIGHT_RIM, 2 * aw), BF16),
            pltpu.VMEM((LEFT_RIM + RIGHT_RIM, 2 * aw), BF16),
            pltpu.VMEM((LEFT_RIM + atoms + RIGHT_RIM, 3 * aw), BF16),
            pltpu.VMEM((atoms, aw), F32),
            pltpu.VMEM((rows, toks, tw), BF16),
            pltpu.VMEM((TH // EACH, 256, EACH * toks), BF16),
            pltpu.VMEM((rows * toks, TH * toks), BF16),
            pltpu.VMEM((tw, toks), F32),
            pltpu.VMEM((1, TH * toks), F32),
            pltpu.VMEM((1, TH * toks), F32),
            pltpu.VMEM((tw // TH, TH * toks), F32),
            pltpu.SemaphoreType.DMA((len(taken),)),
            pltpu.SemaphoreType.DMA((2,)),
            pltpu.SemaphoreType.DMA((2,)),
            pltpu.SemaphoreType.DMA((rows, PIECES, 4)),
            pltpu.SemaphoreType.DMA((rows, PIECES)),
        ],
        compiler_params=pltpu.CompilerParams(collective_id=0, has_side_effects=True),
    )(atom_count, *taken)
    held = [pltpu.with_memory_space_constraint(r, pltpu.VMEM) for r in results]
    return pl.pallas_call(
        hand_on,
        out_shape=tuple(jax.ShapeDtypeStruct(r.shape, r.dtype) for r in results),
        in_specs=(vmem, vmem),
        out_specs=(anywhere, anywhere),
        scratch_shapes=[pltpu.SemaphoreType.DMA((2,))],
    )(*held)


def chips_across(mesh):
    rows = mesh.shape["row"]
    group = mesh.devices.reshape(-1)[:rows]
    places = [getattr(device, "coords", None) for device in group]
    if any(place is None for place in places):
        return 1
    wide = len({place[1] for place in places})
    return 2 if wide == 2 and rows % 4 == 0 else 1


def solution(mesh):
    rows = mesh.shape["row"]
    return jax.shard_map(
        functools.partial(on_device, rows, chips_across(mesh)),
        mesh=mesh,
        in_specs=(
            P(("sample", "row"), None),
            P(),
            P("row"),
            P("row", None, None, None),
            P(("sample", "row"), None),
            P(None, "row", None),
            P(), P(), P(), P(), P(), P(), P(), P(), P(),
        ),
        out_specs=(P(("sample", "row"), None), P(("sample", "row"), None)),
        check_vma=False,
    )
```

```python
import functools

import jax
import jax.numpy as jnp
from jax import lax
from jax.experimental import pallas as pl
from jax.experimental.pallas import tpu as pltpu
from jax.sharding import PartitionSpec as P

TH = 16
AH = 4
WQ = 32
WK = 128
LEFT_RIM = 48
RIGHT_RIM = 80
EPSILON = 1e-05
MASKED = -1000000000.0
PIECES = 2
EACH = 4
F32 = jnp.float32
BF16 = jnp.bfloat16
MESH = pl.DeviceIdType.MESH


def normalized(values, gain):
    floats = values.astype(F32)
    average = jnp.mean(floats, axis=-1, keepdims=True)
    centred = floats - average
    spread = jnp.mean(centred * centred, axis=-1, keepdims=True)
    return (centred * lax.rsqrt(spread + EPSILON) * gain).astype(BF16)


def product(left, right):
    return jnp.dot(left, right, preferred_element_type=F32)


def product_t(left, right):
    return lax.dot_general(left, right, (((1,), (1,)), ((), ())), preferred_element_type=F32)


def iota(shape, dimension):
    return lax.broadcasted_iota(jnp.int32, shape, dimension)


def head_groups(heads, size, each):
    return [(first, min(first * size // 128 * 128, heads * size - 256)) for first in range(0, heads, each)]


def kernel(
    rows, ny,
    count_hbm, x_hbm, again_hbm, qkvg_hbm, abias_hbm, token_hbm, tgain_hbm, aproj_hbm,
    a2t_hbm, tsingle_hbm, tqg_hbm, tkv_hbm, tbias_hbm, tproj_hbm, t2a_hbm,
    aout_ref, tout_ref,
    count_ref, x_ref, again_ref, qkvg_ref, abias, token_ref, tgain_ref, aproj_ref,
    a2t, tsingle, tqg, tkv, tbias, tproj, t2a,
    rims, halo, ext, att, gathered, qbuf, turned_bias, turned_gate, mbuf, lbuf, acc,
    load_sem, halo_send, halo_recv, send_sem, recv_sem,
):
    atoms, aw = x_ref.shape
    toks, tw = tsingle.shape
    ahead = aw // AH
    thead = tw // TH
    me = lax.axis_index("row")
    core = me % 2
    chip = me // 2
    y = chip % ny
    z = chip // ny
    nz = rows // (2 * ny)
    groups = head_groups(TH, thead, EACH)
    wide = EACH * toks

    def index(zz, yy, cc):
        return (zz * ny + yy) * 2 + cc

    sibling = index(z, y, 1 - core)
    other = index(z, 1 - y, core)
    up = index(z + 1, y, core)
    down = index(z - 1, y, core)

    barrier = pltpu.get_barrier_semaphore()

    def greet(target):
        pl.semaphore_signal(barrier, inc=1, device_id={"row": target}, device_id_type=MESH)

    pl.when(me + 1 < rows)(lambda: greet(me + 1))
    pl.when(me > 0)(lambda: greet(me - 1))
    greet(sibling)
    if ny > 1:
        greet(other)
    pl.when(z + 1 < nz)(lambda: greet(up))
    pl.when(z > 0)(lambda: greet(down))

    loads = [
        pltpu.make_async_copy(source, target, load_sem.at[place])
        for place, (source, target) in enumerate(
            (
                (x_hbm, x_ref), (again_hbm, again_ref), (qkvg_hbm, qkvg_ref), (count_hbm, count_ref), (abias_hbm, abias),
                (token_hbm, token_ref), (tgain_hbm, tgain_ref), (aproj_hbm, aproj_ref), (a2t_hbm, a2t),
                (tsingle_hbm, tsingle), (tqg_hbm, tqg), (tkv_hbm, tkv), (tbias_hbm, tbias),
                (tproj_hbm, tproj), (t2a_hbm, t2a),
            )
        )
    ]
    for load in loads[:4]:
        load.start()
    (
        load_x, load_again, load_qkvg, load_count, load_abias, load_token, load_tgain, load_aproj, load_a2t,
        load_tsingle, load_tqg, load_tkv, load_tbias, load_tproj, load_t2a,
    ) = loads


    @pl.when(me == 0)
    def _():
        halo[0:LEFT_RIM, :] = jnp.zeros((LEFT_RIM, 2 * aw), BF16)

    @pl.when(me == rows - 1)
    def _():
        halo[LEFT_RIM:, :] = jnp.zeros((RIGHT_RIM, 2 * aw), BF16)

    load_x.wait()
    load_again.wait()
    load_qkvg.wait()
    for load in loads[4:]:
        load.start()
    x = x_ref[...]
    load_count.wait()
    count = count_ref[me]
    atom_normed = normalized(x, again_ref[...])
    keyval = product(atom_normed, qkvg_ref[:, aw : 3 * aw]).astype(BF16)
    pick = (iota((LEFT_RIM, atoms), 1) == iota((LEFT_RIM, atoms), 0) + (count - LEFT_RIM))
    rims[0:LEFT_RIM, :] = product(pick.astype(F32).astype(BF16), keyval).astype(BF16)
    rims[LEFT_RIM:, :] = keyval[:RIGHT_RIM]

    pl.semaphore_wait(
        barrier,
        1 + (1 if ny > 1 else 0)
        + jnp.where(z + 1 < nz, 1, 0) + jnp.where(z > 0, 1, 0)
        + jnp.where(me + 1 < rows, 1, 0) + jnp.where(me > 0, 1, 0),
    )

    to_next = pltpu.make_async_remote_copy(
        rims.at[pl.ds(0, LEFT_RIM)], halo.at[pl.ds(0, LEFT_RIM)], halo_send.at[0], halo_recv.at[0],
        device_id={"row": me + 1}, device_id_type=MESH,
    )
    to_prior = pltpu.make_async_remote_copy(
        rims.at[pl.ds(LEFT_RIM, RIGHT_RIM)], halo.at[pl.ds(LEFT_RIM, RIGHT_RIM)],
        halo_send.at[1], halo_recv.at[1],
        device_id={"row": me - 1}, device_id_type=MESH,
    )
    pl.when(me + 1 < rows)(to_next.start)
    pl.when(me > 0)(to_prior.start)

    queries = product(atom_normed, qkvg_ref[:, :aw]).astype(BF16)
    gates = jax.nn.sigmoid(product(atom_normed, qkvg_ref[:, 3 * aw :]).astype(BF16).astype(F32))
    blocks = atoms // WQ
    lane_head = iota((AH * WQ, aw), 1) // ahead
    own_head = (lane_head == iota((AH * WQ, aw), 0) // WQ).astype(F32)
    own_head_half = own_head.astype(BF16)
    span = atoms + RIGHT_RIM
    place = iota((span, WK), 0) - count
    chosen = ((place == iota((span, WK), 1) - LEFT_RIM) & (place >= 0)).astype(F32).astype(BF16)
    within = iota((span, 2 * aw), 0) - count
    within = (within >= 0) & (within < RIGHT_RIM)
    base_rows = jnp.concatenate(
        [keyval.astype(F32), jnp.zeros((RIGHT_RIM, 2 * aw), F32)], axis=0
    )
    ext[:, 2 * aw :] = jnp.ones((ext.shape[0], aw), BF16)
    load_abias.wait()
    load_token.wait()
    load_tgain.wait()
    load_aproj.wait()
    load_a2t.wait()
    load_tsingle.wait()
    pl.when(me > 0)(to_next.wait_recv)
    pl.when(me + 1 < rows)(to_prior.wait_recv)
    rim = halo[...]
    moved = product(chosen, rim)
    ext[0:LEFT_RIM, : 2 * aw] = rim[:LEFT_RIM]
    ext[LEFT_RIM:, : 2 * aw] = jnp.where(within, moved, base_rows).astype(BF16)

    is_first = me == 0
    is_last = me == rows - 1
    low = jnp.where(is_first, 0, -LEFT_RIM)
    high = jnp.where(is_last, count, atoms + WK)
    for start_at in range(0, blocks, 8):
        batch = range(start_at, min(start_at + 8, blocks))
        scores = []
        for w in batch:
            q = queries[w * WQ : (w + 1) * WQ]
            stacked = jnp.concatenate([q] * AH, axis=0) * own_head_half
            scores.append(product_t(stacked, ext[w * WQ : w * WQ + WK, :aw]))
        for at, w in enumerate(batch):
            value = scores[at] * ahead ** (-0.5) + abias[w].reshape(AH * WQ, WK).astype(F32)
            offset = iota((AH * WQ, WK), 1) + (WQ * w - LEFT_RIM)
            scores[at] = jnp.where((offset >= low) & (offset < high), value, MASKED)
        tops = [jnp.max(value, axis=-1, keepdims=True) for value in scores]
        raised = [jnp.exp(value - top) for value, top in zip(scores, tops)]
        results = [
            product(raised[at].astype(BF16), ext[w * WQ : w * WQ + WK, aw:])
            for at, w in enumerate(batch)
        ]
        for at, w in enumerate(batch):
            result = results[at][:, :aw] * own_head / results[at][:, aw:]
            att[w * WQ : (w + 1) * WQ, :] = jnp.sum(result.reshape(AH, WQ, aw), axis=0)
    gated = (att[...] * gates).astype(BF16)
    atom_mid = (x.astype(F32) + product(gated, aproj_ref[...])).astype(BF16)
    lifted = jnp.maximum(product(atom_mid, a2t[...]), 0.0).astype(BF16)
    member = (token_ref[...] == iota((toks, atoms), 0)) & (iota((toks, atoms), 1) < count)
    member_f = member.astype(F32)
    summed = product(member_f.astype(BF16), lifted)
    counts = jnp.sum(member_f, axis=1, keepdims=True)
    hidden = tsingle[...].astype(F32) + summed / counts
    normed = normalized(hidden, tgain_ref[...].reshape(1, tw))
    gathered[me] = normed

    piece_rows = toks // PIECES

    def copy(source, piece, way, target):
        view = gathered.at[source, pl.ds(piece * piece_rows, piece_rows)]
        return pltpu.make_async_remote_copy(
            view, view, send_sem.at[source, piece, way], recv_sem.at[source, piece],
            device_id={"row": target}, device_id_type=MESH,
        )

    def pass_up(source, piece, act):
        pl.when(z + 1 < nz)(lambda: act(copy(source, piece, 2, up)))

    def pass_down(source, piece, act):
        pl.when(z > 0)(lambda: act(copy(source, piece, 3, down)))

    def pass_near(source, piece, act):
        if ny > 1:
            act(copy(source, piece, 1, other))
        act(copy(source, piece, 0, sibling))

    start = lambda c: c.start()
    sent = lambda c: c.wait_send()

    def arrived(source, piece):
        copy(source, piece, 0, sibling).wait_recv()

    def own(act):
        for piece in range(PIECES):
            pass_up(me, piece, act)
            pass_down(me, piece, act)
            pass_near(me, piece, act)

    def along_z(distance, act, wait):
        for piece in range(PIECES):
            @pl.when(z - distance >= 0)
            def _():
                source = index(z - distance, y, core)
                if wait:
                    arrived(source, piece)
                pass_up(source, piece, act)
                pass_near(source, piece, act)

            @pl.when(z + distance < nz)
            def _():
                source = index(z + distance, y, core)
                if wait:
                    arrived(source, piece)
                pass_down(source, piece, act)
                pass_near(source, piece, act)

    def along_y(distance, act, wait):
        if ny == 1:
            return
        for piece in range(PIECES):
            for sign in (-1, 1):
                zz = z + sign * distance

                @pl.when((zz >= 0) & (zz < nz) & ((sign < 0) | (distance > 0)))
                def _():
                    source = index(zz, 1 - y, core)
                    if wait:
                        arrived(source, piece)
                    act(copy(source, piece, 0, sibling))

    own(start)
    turned = jnp.concatenate([member_f, member_f], axis=0).T.astype(BF16)

    load_tqg.wait()
    qgate = product(normed, tqg[...]).astype(BF16)
    turned_gate[...] = jax.nn.sigmoid(qgate[:, tw:].T.astype(F32))
    for group, (first, base) in enumerate(groups):
        part = qgate[:, base : base + 256].astype(F32)
        lanes = iota(part.shape, 1) + base
        spread_out = []
        for head in range(first, first + EACH):
            keep = (lanes >= head * thead) & (lanes < (head + 1) * thead)
            spread_out.append(jnp.where(keep, part, 0.0).astype(BF16))
        qbuf[group] = jnp.concatenate(spread_out, axis=0).T
    mbuf[...] = jnp.full(mbuf.shape, -jnp.inf, F32)
    lbuf[...] = jnp.zeros(lbuf.shape, F32)
    acc[...] = jnp.zeros(acc.shape, F32)
    load_tkv.wait()
    load_tbias.wait()

    def turn_bias(block, carry):
        keys = pl.ds(pl.multiple_of(block * 2 * toks, 2 * toks), 2 * toks)
        turned_bias[keys, :] = tbias[:, :, keys].reshape(TH * toks, 2 * toks).T
        return carry

    lax.fori_loop(0, rows // 2, turn_bias, 0)
    low_half = iota((thead, wide // 2), 1) < toks

    def attend(block):
        inputs = gathered[pl.ds(2 * block, 2)].reshape(2 * toks, tw)
        kv = product(inputs, tkv[...]).astype(BF16)
        turned_values = kv[:, tw:].T
        keys = pl.ds(pl.multiple_of(block * 2 * toks, 2 * toks), 2 * toks)
        scores = jnp.concatenate(
            [product(kv[:, base : base + 256], qbuf[group]) for group, (first, base) in enumerate(groups)], axis=1
        )
        scores = scores * thead ** (-0.5) + turned_bias[keys, :].astype(F32)
        old = mbuf[...]
        new = jnp.maximum(old, jnp.max(scores, axis=0, keepdims=True))
        factor = jnp.exp(old - new)
        raised = jnp.exp(scores - new)
        mbuf[...] = new
        lbuf[...] = lbuf[...] * factor + jnp.sum(raised, axis=0, keepdims=True)
        weights = raised.astype(BF16)
        updates = [
            product(turned_values[first * thead : (first + EACH) * thead], weights[:, group * wide : (group + 1) * wide])
            for group, (first, base) in enumerate(groups)
        ]
        both = []
        for update in updates:
            for half in range(EACH // 2):
                lanes = slice(half * 2 * toks, (half + 1) * 2 * toks)
                top = 2 * half * thead
                both.append(jnp.where(low_half, update[top : top + thead, lanes], update[top + thead : top + 2 * thead, lanes]))
        acc[...] = acc[...] * factor + jnp.concatenate(both, axis=1)

    def step(t, carry):
        distance = t // (2 * ny)
        turn = t % (2 * ny)

        @pl.when(turn == 0)
        def _():
            along_z(distance + 1, start, True)

        @pl.when(turn == 1)
        def _():
            along_y(distance, start, True)

        yy = jnp.where(turn // 2 == 0, y, 1 - y)
        sign = turn % 2
        zz = z + (2 * sign - 1) * distance

        @pl.when((zz >= 0) & (zz < nz) & ((sign == 0) | (distance > 0)))
        def _():
            for piece in range(PIECES):
                arrived(index(zz, yy, 1 - core), piece)
            attend(zz * ny + yy)

        return carry

    lax.fori_loop(0, nz * 2 * ny, step, 0)

    whole = acc[...] / lbuf[...]
    columns = [whole[:, head * toks : (head + 1) * toks] for head in range(TH)]
    attended = jnp.concatenate(columns, axis=0)
    tok_gated = (attended * turned_gate[...]).astype(BF16).T
    load_tproj.wait()
    token_out = (hidden + product(tok_gated, tproj[...])).astype(BF16)
    tout_ref[...] = token_out
    load_t2a.wait()
    back = product(token_out, t2a[...])
    high_part = back.astype(BF16)
    rest = back - high_part.astype(F32)
    spread = product(turned, jnp.concatenate([high_part, rest.astype(BF16)], axis=0))
    live = iota((atoms, aw), 0) < count
    aout_ref[...] = jnp.where(live, atom_mid.astype(F32) + spread, 0.0).astype(BF16)

    pl.when(me + 1 < rows)(to_next.wait_send)
    pl.when(me > 0)(to_prior.wait_send)
    own(sent)

    def drain(distance, carry):
        along_z(distance, sent, False)
        along_y(distance - 1, sent, False)
        return carry

    lax.fori_loop(1, nz, drain, 0)
    along_y(nz - 1, sent, False)


def hand_on(a_ref, t_ref, aout_ref, tout_ref, sem):
    copies = [
        pltpu.make_async_copy(a_ref, aout_ref, sem.at[0]),
        pltpu.make_async_copy(t_ref, tout_ref, sem.at[1]),
    ]
    for copy in copies:
        copy.start()
    for copy in copies:
        copy.wait()


def on_device(
    rows, ny, atom_single, atom_count, atom_token, atom_bias, token_single, token_bias,
    atom_gain, atom_qkvg, atom_proj, atom_to_token, token_gain, token_qg, token_kv,
    token_proj, token_to_atom,
):
    atoms, aw = atom_single.shape
    toks, tw = token_single.shape
    vmem = pl.BlockSpec(memory_space=pltpu.VMEM)
    anywhere = pl.BlockSpec(memory_space=pl.ANY)
    taken = [
        atom_single, atom_gain.reshape(1, aw), atom_qkvg, atom_bias, atom_token.reshape(1, atoms), token_gain,
        atom_proj, atom_to_token, token_single, token_qg, token_kv, token_bias, token_proj, token_to_atom,
    ]
    results = pl.pallas_call(
        functools.partial(kernel, rows, ny),
        out_shape=(pltpu.VMEM((atoms, aw), BF16), pltpu.VMEM((toks, tw), BF16)),
        in_specs=[anywhere] * (1 + len(taken)),
        out_specs=(vmem, vmem),
        scratch_shapes=[pltpu.SMEM(atom_count.shape, atom_count.dtype)]
        + [pltpu.VMEM(a.shape, a.dtype) for a in taken]
        + [
            pltpu.VMEM((LEFT_RIM + RIGHT_RIM, 2 * aw), BF16),
            pltpu.VMEM((LEFT_RIM + RIGHT_RIM, 2 * aw), BF16),
            pltpu.VMEM((LEFT_RIM + atoms + RIGHT_RIM, 3 * aw), BF16),
            pltpu.VMEM((atoms, aw), F32),
            pltpu.VMEM((rows, toks, tw), BF16),
            pltpu.VMEM((TH // EACH, 256, EACH * toks), BF16),
            pltpu.VMEM((rows * toks, TH * toks), BF16),
            pltpu.VMEM((tw, toks), F32),
            pltpu.VMEM((1, TH * toks), F32),
            pltpu.VMEM((1, TH * toks), F32),
            pltpu.VMEM((tw // TH, TH * toks), F32),
            pltpu.SemaphoreType.DMA((1 + len(taken),)),
            pltpu.SemaphoreType.DMA((2,)),
            pltpu.SemaphoreType.DMA((2,)),
            pltpu.SemaphoreType.DMA((rows, PIECES, 4)),
            pltpu.SemaphoreType.DMA((rows, PIECES)),
        ],
        compiler_params=pltpu.CompilerParams(collective_id=0, has_side_effects=True),
    )(atom_count, *taken)
    held = [pltpu.with_memory_space_constraint(r, pltpu.VMEM) for r in results]
    return pl.pallas_call(
        hand_on,
        out_shape=tuple(jax.ShapeDtypeStruct(r.shape, r.dtype) for r in results),
        in_specs=(vmem, vmem),
        out_specs=(anywhere, anywhere),
        scratch_shapes=[pltpu.SemaphoreType.DMA((2,))],
    )(*held)


def chips_across(mesh):
    rows = mesh.shape["row"]
    group = mesh.devices.reshape(-1)[:rows]
    places = [getattr(device, "coords", None) for device in group]
    if any(place is None for place in places):
        return 1
    wide = len({place[1] for place in places})
    return 2 if wide == 2 and rows % 4 == 0 else 1


def solution(mesh):
    rows = mesh.shape["row"]
    return jax.shard_map(
        functools.partial(on_device, rows, chips_across(mesh)),
        mesh=mesh,
        in_specs=(
            P(("sample", "row"), None),
            P(),
            P("row"),
            P("row", None, None, None),
            P(("sample", "row"), None),
            P(None, "row", None),
            P(), P(), P(), P(), P(), P(), P(), P(), P(),
        ),
        out_specs=(P(("sample", "row"), None), P(("sample", "row"), None)),
        check_vma=False,
    )
```

```python
import functools

import jax
import jax.numpy as jnp
from jax import lax
from jax.experimental import pallas as pl
from jax.experimental.pallas import tpu as pltpu
from jax.sharding import PartitionSpec as P

TH = 16
AH = 4
WQ = 32
WK = 128
LEFT_RIM = 48
RIGHT_RIM = 80
EPSILON = 1e-05
MASKED = -1000000000.0
PIECES = 2
EACH = 4
F32 = jnp.float32
BF16 = jnp.bfloat16
MESH = pl.DeviceIdType.MESH


def normalized(values, gain):
    floats = values.astype(F32)
    average = jnp.mean(floats, axis=-1, keepdims=True)
    centred = floats - average
    spread = jnp.mean(centred * centred, axis=-1, keepdims=True)
    return (centred * lax.rsqrt(spread + EPSILON) * gain).astype(BF16)


def product(left, right):
    return jnp.dot(left, right, preferred_element_type=F32)


def product_t(left, right):
    return lax.dot_general(left, right, (((1,), (1,)), ((), ())), preferred_element_type=F32)


def iota(shape, dimension):
    return lax.broadcasted_iota(jnp.int32, shape, dimension)


def head_groups(heads, size, each):
    return [(first, min(first * size // 128 * 128, heads * size - 256)) for first in range(0, heads, each)]


def kernel(
    rows, ny,
    count_hbm, x_hbm, again_hbm, qkvg_hbm, abias_hbm, token_hbm, tgain_hbm, aproj_hbm,
    a2t_hbm, tsingle_hbm, tqg_hbm, tkv_hbm, tbias_hbm, tproj_hbm, t2a_hbm,
    aout_ref, tout_ref,
    count_ref, x_ref, again_ref, qkvg_ref, abias, token_ref, tgain_ref, aproj_ref,
    a2t, tsingle, tqg, tkv, tbias, tproj, t2a,
    rims, halo, ext, att, gathered, qbuf, turned_bias, turned_gate, mbuf, lbuf, acc,
    load_sem, halo_send, halo_recv, send_sem, recv_sem,
):
    atoms, aw = x_ref.shape
    toks, tw = tsingle.shape
    ahead = aw // AH
    thead = tw // TH
    me = lax.axis_index("row")
    core = me % 2
    chip = me // 2
    y = chip % ny
    z = chip // ny
    nz = rows // (2 * ny)
    groups = head_groups(TH, thead, EACH)
    wide = EACH * toks

    def index(zz, yy, cc):
        return (zz * ny + yy) * 2 + cc

    sibling = index(z, y, 1 - core)
    other = index(z, 1 - y, core)
    up = index(z + 1, y, core)
    down = index(z - 1, y, core)

    barrier = pltpu.get_barrier_semaphore()

    def greet(target):
        pl.semaphore_signal(barrier, inc=1, device_id={"row": target}, device_id_type=MESH)

    pl.when(me + 1 < rows)(lambda: greet(me + 1))
    pl.when(me > 0)(lambda: greet(me - 1))
    greet(sibling)
    if ny > 1:
        greet(other)
    pl.when(z + 1 < nz)(lambda: greet(up))
    pl.when(z > 0)(lambda: greet(down))

    loads = [
        pltpu.make_async_copy(source, target, load_sem.at[place])
        for place, (source, target) in enumerate(
            (
                (x_hbm, x_ref), (again_hbm, again_ref), (qkvg_hbm, qkvg_ref), (count_hbm, count_ref), (abias_hbm, abias),
                (token_hbm, token_ref), (tgain_hbm, tgain_ref), (aproj_hbm, aproj_ref), (a2t_hbm, a2t),
                (tsingle_hbm, tsingle), (tqg_hbm, tqg), (tkv_hbm, tkv), (tbias_hbm, tbias),
                (tproj_hbm, tproj), (t2a_hbm, t2a),
            )
        )
    ]
    for load in loads[:4]:
        load.start()
    (
        load_x, load_again, load_qkvg, load_count, load_abias, load_token, load_tgain, load_aproj, load_a2t,
        load_tsingle, load_tqg, load_tkv, load_tbias, load_tproj, load_t2a,
    ) = loads


    @pl.when(me == 0)
    def _():
        halo[0:LEFT_RIM, :] = jnp.zeros((LEFT_RIM, 2 * aw), BF16)

    @pl.when(me == rows - 1)
    def _():
        halo[LEFT_RIM:, :] = jnp.zeros((RIGHT_RIM, 2 * aw), BF16)

    load_x.wait()
    load_again.wait()
    load_qkvg.wait()
    for load in loads[4:]:
        load.start()
    x = x_ref[...]
    load_count.wait()
    count = count_ref[me]
    atom_normed = normalized(x, again_ref[...])
    keyval = product(atom_normed, qkvg_ref[:, aw : 3 * aw]).astype(BF16)
    pick = (iota((LEFT_RIM, atoms), 1) == iota((LEFT_RIM, atoms), 0) + (count - LEFT_RIM))
    rims[0:LEFT_RIM, :] = product(pick.astype(F32).astype(BF16), keyval).astype(BF16)
    rims[LEFT_RIM:, :] = keyval[:RIGHT_RIM]

    pl.semaphore_wait(
        barrier,
        1 + (1 if ny > 1 else 0)
        + jnp.where(z + 1 < nz, 1, 0) + jnp.where(z > 0, 1, 0)
        + jnp.where(me + 1 < rows, 1, 0) + jnp.where(me > 0, 1, 0),
    )

    to_next = pltpu.make_async_remote_copy(
        rims.at[pl.ds(0, LEFT_RIM)], halo.at[pl.ds(0, LEFT_RIM)], halo_send.at[0], halo_recv.at[0],
        device_id={"row": me + 1}, device_id_type=MESH,
    )
    to_prior = pltpu.make_async_remote_copy(
        rims.at[pl.ds(LEFT_RIM, RIGHT_RIM)], halo.at[pl.ds(LEFT_RIM, RIGHT_RIM)],
        halo_send.at[1], halo_recv.at[1],
        device_id={"row": me - 1}, device_id_type=MESH,
    )
    pl.when(me + 1 < rows)(to_next.start)
    pl.when(me > 0)(to_prior.start)

    queries = product(atom_normed, qkvg_ref[:, :aw]).astype(BF16)
    gates = jax.nn.sigmoid(product(atom_normed, qkvg_ref[:, 3 * aw :]).astype(BF16).astype(F32))
    blocks = atoms // WQ
    lane_head = iota((AH * WQ, aw), 1) // ahead
    own_head = (lane_head == iota((AH * WQ, aw), 0) // WQ).astype(F32)
    own_head_half = own_head.astype(BF16)
    own_heads = jnp.concatenate([own_head, own_head], axis=1)
    span = atoms + RIGHT_RIM
    place = iota((span, WK), 0) - count
    chosen = ((place == iota((span, WK), 1) - LEFT_RIM) & (place >= 0)).astype(F32).astype(BF16)
    within = iota((span, 2 * aw), 0) - count
    within = (within >= 0) & (within < RIGHT_RIM)
    base_rows = jnp.concatenate(
        [keyval.astype(F32), jnp.zeros((RIGHT_RIM, 2 * aw), F32)], axis=0
    )
    ext[:, 2 * aw :] = jnp.ones((ext.shape[0], aw), BF16)
    load_abias.wait()
    load_token.wait()
    load_tgain.wait()
    load_aproj.wait()
    load_a2t.wait()
    load_tsingle.wait()
    pl.when(me > 0)(to_next.wait_recv)
    pl.when(me + 1 < rows)(to_prior.wait_recv)
    rim = halo[...]
    moved = product(chosen, rim)
    ext[0:LEFT_RIM, : 2 * aw] = rim[:LEFT_RIM]
    ext[LEFT_RIM:, : 2 * aw] = jnp.where(within, moved, base_rows).astype(BF16)

    is_first = me == 0
    is_last = me == rows - 1
    low = jnp.where(is_first, 0, -LEFT_RIM)
    high = jnp.where(is_last, count, atoms + WK)
    for start_at in range(0, blocks, 8):
        batch = range(start_at, min(start_at + 8, blocks))
        scores = []
        for w in batch:
            q = queries[w * WQ : (w + 1) * WQ]
            stacked = jnp.concatenate([q] * AH, axis=0) * own_head_half
            scores.append(product_t(stacked, ext[w * WQ : w * WQ + WK, :aw]))
        for at, w in enumerate(batch):
            value = scores[at] * ahead ** (-0.5) + abias[w].reshape(AH * WQ, WK).astype(F32)
            offset = iota((AH * WQ, WK), 1) + (WQ * w - LEFT_RIM)
            scores[at] = jnp.where((offset >= low) & (offset < high), value, MASKED)
        tops = [jnp.max(value, axis=-1, keepdims=True) for value in scores]
        raised = [jnp.exp(value - top) for value, top in zip(scores, tops)]
        results = [
            product(raised[at].astype(BF16), ext[w * WQ : w * WQ + WK, aw:])
            for at, w in enumerate(batch)
        ]
        for at, w in enumerate(batch):
            result = results[at] * own_heads
            att[w * WQ : (w + 1) * WQ, :] = jnp.sum(result.reshape(AH, WQ, 2 * aw), axis=0)
    gated = (att[:, :aw] / att[:, aw:] * gates).astype(BF16)
    atom_mid = (x.astype(F32) + product(gated, aproj_ref[...])).astype(BF16)
    lifted = jnp.maximum(product(atom_mid, a2t[...]), 0.0).astype(BF16)
    member = (token_ref[...] == iota((toks, atoms), 0)) & (iota((toks, atoms), 1) < count)
    member_f = member.astype(F32)
    summed = product(member_f.astype(BF16), lifted)
    counts = jnp.sum(member_f, axis=1, keepdims=True)
    hidden = tsingle[...].astype(F32) + summed / counts
    normed = normalized(hidden, tgain_ref[...].reshape(1, tw))
    gathered[me] = normed

    piece_rows = toks // PIECES

    def copy(source, piece, way, target):
        view = gathered.at[source, pl.ds(piece * piece_rows, piece_rows)]
        return pltpu.make_async_remote_copy(
            view, view, send_sem.at[source, piece, way], recv_sem.at[source, piece],
            device_id={"row": target}, device_id_type=MESH,
        )

    def pass_up(source, piece, act):
        pl.when(z + 1 < nz)(lambda: act(copy(source, piece, 2, up)))

    def pass_down(source, piece, act):
        pl.when(z > 0)(lambda: act(copy(source, piece, 3, down)))

    def pass_near(source, piece, act):
        if ny > 1:
            act(copy(source, piece, 1, other))
        act(copy(source, piece, 0, sibling))

    start = lambda c: c.start()
    sent = lambda c: c.wait_send()

    def arrived(source, piece):
        copy(source, piece, 0, sibling).wait_recv()

    def own(act):
        for piece in range(PIECES):
            pass_up(me, piece, act)
            pass_down(me, piece, act)
            pass_near(me, piece, act)

    def along_z(distance, act, wait):
        for piece in range(PIECES):
            @pl.when(z - distance >= 0)
            def _():
                source = index(z - distance, y, core)
                if wait:
                    arrived(source, piece)
                pass_up(source, piece, act)
                pass_near(source, piece, act)

            @pl.when(z + distance < nz)
            def _():
                source = index(z + distance, y, core)
                if wait:
                    arrived(source, piece)
                pass_down(source, piece, act)
                pass_near(source, piece, act)

    def along_y(distance, act, wait):
        if ny == 1:
            return
        for piece in range(PIECES):
            for sign in (-1, 1):
                zz = z + sign * distance

                @pl.when((zz >= 0) & (zz < nz) & ((sign < 0) | (distance > 0)))
                def _():
                    source = index(zz, 1 - y, core)
                    if wait:
                        arrived(source, piece)
                    act(copy(source, piece, 0, sibling))

    own(start)
    turned = jnp.concatenate([member_f, member_f], axis=0).T.astype(BF16)

    load_tqg.wait()
    qgate = product(normed, tqg[...]).astype(BF16)
    turned_gate[...] = jax.nn.sigmoid(qgate[:, tw:].T.astype(F32))
    for group, (first, base) in enumerate(groups):
        part = qgate[:, base : base + 256].astype(F32)
        lanes = iota(part.shape, 1) + base
        spread_out = []
        for head in range(first, first + EACH):
            keep = (lanes >= head * thead) & (lanes < (head + 1) * thead)
            spread_out.append(jnp.where(keep, part, 0.0).astype(BF16))
        qbuf[group] = jnp.concatenate(spread_out, axis=0).T
    mbuf[...] = jnp.full(mbuf.shape, -jnp.inf, F32)
    lbuf[...] = jnp.zeros(lbuf.shape, F32)
    acc[...] = jnp.zeros(acc.shape, F32)
    load_tkv.wait()
    load_tbias.wait()

    def turn_bias(block, carry):
        keys = pl.ds(pl.multiple_of(block * 2 * toks, 2 * toks), 2 * toks)
        turned_bias[keys, :] = tbias[:, :, keys].reshape(TH * toks, 2 * toks).T
        return carry

    lax.fori_loop(0, rows // 2, turn_bias, 0)
    low_half = iota((thead, wide // 2), 1) < toks

    def attend(block):
        inputs = gathered[pl.ds(2 * block, 2)].reshape(2 * toks, tw)
        kv = product(inputs, tkv[...]).astype(BF16)
        turned_values = kv[:, tw:].T
        keys = pl.ds(pl.multiple_of(block * 2 * toks, 2 * toks), 2 * toks)
        scores = jnp.concatenate(
            [product(kv[:, base : base + 256], qbuf[group]) for group, (first, base) in enumerate(groups)], axis=1
        )
        scores = scores * thead ** (-0.5) + turned_bias[keys, :].astype(F32)
        old = mbuf[...]
        new = jnp.maximum(old, jnp.max(scores, axis=0, keepdims=True))
        factor = jnp.exp(old - new)
        raised = jnp.exp(scores - new)
        mbuf[...] = new
        lbuf[...] = lbuf[...] * factor + jnp.sum(raised, axis=0, keepdims=True)
        weights = raised.astype(BF16)
        updates = [
            product(turned_values[first * thead : (first + EACH) * thead], weights[:, group * wide : (group + 1) * wide])
            for group, (first, base) in enumerate(groups)
        ]
        both = []
        for update in updates:
            for half in range(EACH // 2):
                lanes = slice(half * 2 * toks, (half + 1) * 2 * toks)
                top = 2 * half * thead
                both.append(jnp.where(low_half, update[top : top + thead, lanes], update[top + thead : top + 2 * thead, lanes]))
        acc[...] = acc[...] * factor + jnp.concatenate(both, axis=1)

    def step(t, carry):
        distance = t // (2 * ny)
        turn = t % (2 * ny)

        @pl.when(turn == 0)
        def _():
            along_z(distance + 1, start, True)

        @pl.when(turn == 1)
        def _():
            along_y(distance, start, True)

        yy = jnp.where(turn // 2 == 0, y, 1 - y)
        sign = turn % 2
        zz = z + (2 * sign - 1) * distance

        @pl.when((zz >= 0) & (zz < nz) & ((sign == 0) | (distance > 0)))
        def _():
            for piece in range(PIECES):
                arrived(index(zz, yy, 1 - core), piece)
            attend(zz * ny + yy)

        return carry

    lax.fori_loop(0, nz * 2 * ny, step, 0)

    whole = acc[...] / lbuf[...]
    columns = [whole[:, head * toks : (head + 1) * toks] for head in range(TH)]
    attended = jnp.concatenate(columns, axis=0)
    tok_gated = (attended * turned_gate[...]).astype(BF16).T
    load_tproj.wait()
    token_out = (hidden + product(tok_gated, tproj[...])).astype(BF16)
    tout_ref[...] = token_out
    load_t2a.wait()
    back = product(token_out, t2a[...])
    high_part = back.astype(BF16)
    rest = back - high_part.astype(F32)
    spread = product(turned, jnp.concatenate([high_part, rest.astype(BF16)], axis=0))
    live = iota((atoms, aw), 0) < count
    aout_ref[...] = jnp.where(live, atom_mid.astype(F32) + spread, 0.0).astype(BF16)

    pl.when(me + 1 < rows)(to_next.wait_send)
    pl.when(me > 0)(to_prior.wait_send)
    own(sent)

    def drain(distance, carry):
        along_z(distance, sent, False)
        along_y(distance - 1, sent, False)
        return carry

    lax.fori_loop(1, nz, drain, 0)
    along_y(nz - 1, sent, False)


def hand_on(a_ref, t_ref, aout_ref, tout_ref, sem):
    copies = [
        pltpu.make_async_copy(a_ref, aout_ref, sem.at[0]),
        pltpu.make_async_copy(t_ref, tout_ref, sem.at[1]),
    ]
    for copy in copies:
        copy.start()
    for copy in copies:
        copy.wait()


def on_device(
    rows, ny, atom_single, atom_count, atom_token, atom_bias, token_single, token_bias,
    atom_gain, atom_qkvg, atom_proj, atom_to_token, token_gain, token_qg, token_kv,
    token_proj, token_to_atom,
):
    atoms, aw = atom_single.shape
    toks, tw = token_single.shape
    vmem = pl.BlockSpec(memory_space=pltpu.VMEM)
    anywhere = pl.BlockSpec(memory_space=pl.ANY)
    taken = [
        atom_single, atom_gain.reshape(1, aw), atom_qkvg, atom_bias, atom_token.reshape(1, atoms), token_gain,
        atom_proj, atom_to_token, token_single, token_qg, token_kv, token_bias, token_proj, token_to_atom,
    ]
    results = pl.pallas_call(
        functools.partial(kernel, rows, ny),
        out_shape=(pltpu.VMEM((atoms, aw), BF16), pltpu.VMEM((toks, tw), BF16)),
        in_specs=[anywhere] * (1 + len(taken)),
        out_specs=(vmem, vmem),
        scratch_shapes=[pltpu.SMEM(atom_count.shape, atom_count.dtype)]
        + [pltpu.VMEM(a.shape, a.dtype) for a in taken]
        + [
            pltpu.VMEM((LEFT_RIM + RIGHT_RIM, 2 * aw), BF16),
            pltpu.VMEM((LEFT_RIM + RIGHT_RIM, 2 * aw), BF16),
            pltpu.VMEM((LEFT_RIM + atoms + RIGHT_RIM, 3 * aw), BF16),
            pltpu.VMEM((atoms, 2 * aw), F32),
            pltpu.VMEM((rows, toks, tw), BF16),
            pltpu.VMEM((TH // EACH, 256, EACH * toks), BF16),
            pltpu.VMEM((rows * toks, TH * toks), BF16),
            pltpu.VMEM((tw, toks), F32),
            pltpu.VMEM((1, TH * toks), F32),
            pltpu.VMEM((1, TH * toks), F32),
            pltpu.VMEM((tw // TH, TH * toks), F32),
            pltpu.SemaphoreType.DMA((1 + len(taken),)),
            pltpu.SemaphoreType.DMA((2,)),
            pltpu.SemaphoreType.DMA((2,)),
            pltpu.SemaphoreType.DMA((rows, PIECES, 4)),
            pltpu.SemaphoreType.DMA((rows, PIECES)),
        ],
        compiler_params=pltpu.CompilerParams(collective_id=0, has_side_effects=True),
    )(atom_count, *taken)
    held = [pltpu.with_memory_space_constraint(r, pltpu.VMEM) for r in results]
    return pl.pallas_call(
        hand_on,
        out_shape=tuple(jax.ShapeDtypeStruct(r.shape, r.dtype) for r in results),
        in_specs=(vmem, vmem),
        out_specs=(anywhere, anywhere),
        scratch_shapes=[pltpu.SemaphoreType.DMA((2,))],
    )(*held)


def chips_across(mesh):
    rows = mesh.shape["row"]
    group = mesh.devices.reshape(-1)[:rows]
    places = [getattr(device, "coords", None) for device in group]
    if any(place is None for place in places):
        return 1
    wide = len({place[1] for place in places})
    return 2 if wide == 2 and rows % 4 == 0 else 1


def solution(mesh):
    rows = mesh.shape["row"]
    return jax.shard_map(
        functools.partial(on_device, rows, chips_across(mesh)),
        mesh=mesh,
        in_specs=(
            P(("sample", "row"), None),
            P(),
            P("row"),
            P("row", None, None, None),
            P(("sample", "row"), None),
            P(None, "row", None),
            P(), P(), P(), P(), P(), P(), P(), P(), P(),
        ),
        out_specs=(P(("sample", "row"), None), P(("sample", "row"), None)),
        check_vma=False,
    )
```

```python
import functools

import jax
import jax.numpy as jnp
from jax import lax
from jax.experimental import pallas as pl
from jax.experimental.pallas import tpu as pltpu
from jax.sharding import PartitionSpec as P

TH = 16
AH = 4
WQ = 32
WK = 128
LEFT_RIM = 48
RIGHT_RIM = 80
EPSILON = 1e-05
MASKED = -1000000000.0
PIECES = 2
EACH = 4
F32 = jnp.float32
BF16 = jnp.bfloat16
MESH = pl.DeviceIdType.MESH


def normalized(values, gain):
    floats = values.astype(F32)
    average = jnp.mean(floats, axis=-1, keepdims=True)
    centred = floats - average
    spread = jnp.mean(centred * centred, axis=-1, keepdims=True)
    return (centred * lax.rsqrt(spread + EPSILON) * gain).astype(BF16)


def product(left, right):
    return jnp.dot(left, right, preferred_element_type=F32)


def product_t(left, right):
    return lax.dot_general(left, right, (((1,), (1,)), ((), ())), preferred_element_type=F32)


def iota(shape, dimension):
    return lax.broadcasted_iota(jnp.int32, shape, dimension)


def head_groups(heads, size, each):
    return [(first, min(first * size // 128 * 128, heads * size - 256)) for first in range(0, heads, each)]


def kernel(
    rows, ny,
    count_hbm, x_hbm, again_hbm, qkvg_hbm, abias_hbm, token_hbm, tgain_hbm, aproj_hbm,
    a2t_hbm, tsingle_hbm, tqg_hbm, tkv_hbm, tbias_hbm, tproj_hbm, t2a_hbm,
    aout_ref, tout_ref,
    count_ref, x_ref, again_ref, qkvg_ref, abias, token_ref, tgain_ref, aproj_ref,
    a2t, tsingle, tqg, tkv, tbias, tproj, t2a,
    rims, halo, ext, att, gathered, qbuf, turned_bias, turned_gate, mbuf, lbuf, acc,
    load_sem, halo_send, halo_recv, send_sem, recv_sem,
):
    atoms, aw = x_ref.shape
    toks, tw = tsingle.shape
    ahead = aw // AH
    thead = tw // TH
    me = lax.axis_index("row")
    core = me % 2
    chip = me // 2
    y = chip % ny
    z = chip // ny
    nz = rows // (2 * ny)
    groups = head_groups(TH, thead, EACH)
    wide = EACH * toks

    def index(zz, yy, cc):
        return (zz * ny + yy) * 2 + cc

    sibling = index(z, y, 1 - core)
    other = index(z, 1 - y, core)
    up = index(z + 1, y, core)
    down = index(z - 1, y, core)

    barrier = pltpu.get_barrier_semaphore()

    def greet(target):
        pl.semaphore_signal(barrier, inc=1, device_id={"row": target}, device_id_type=MESH)

    pl.when(me + 1 < rows)(lambda: greet(me + 1))
    pl.when(me > 0)(lambda: greet(me - 1))
    greet(sibling)
    if ny > 1:
        greet(other)
    pl.when(z + 1 < nz)(lambda: greet(up))
    pl.when(z > 0)(lambda: greet(down))

    loads = [
        pltpu.make_async_copy(source, target, load_sem.at[place])
        for place, (source, target) in enumerate(
            (
                (x_hbm, x_ref), (again_hbm, again_ref), (qkvg_hbm, qkvg_ref), (count_hbm, count_ref), (abias_hbm, abias),
                (token_hbm, token_ref), (tgain_hbm, tgain_ref), (aproj_hbm, aproj_ref), (a2t_hbm, a2t),
                (tsingle_hbm, tsingle), (tqg_hbm, tqg), (tkv_hbm, tkv), (tbias_hbm, tbias),
                (tproj_hbm, tproj), (t2a_hbm, t2a),
            )
        )
    ]
    for load in loads[:4]:
        load.start()
    (
        load_x, load_again, load_qkvg, load_count, load_abias, load_token, load_tgain, load_aproj, load_a2t,
        load_tsingle, load_tqg, load_tkv, load_tbias, load_tproj, load_t2a,
    ) = loads


    @pl.when(me == 0)
    def _():
        halo[0:LEFT_RIM, :] = jnp.zeros((LEFT_RIM, 2 * aw), BF16)

    @pl.when(me == rows - 1)
    def _():
        halo[LEFT_RIM:, :] = jnp.zeros((RIGHT_RIM, 2 * aw), BF16)

    load_x.wait()
    load_again.wait()
    load_qkvg.wait()
    for load in loads[4:10]:
        load.start()
    x = x_ref[...]
    load_count.wait()
    count = count_ref[me]
    atom_normed = normalized(x, again_ref[...])
    keyval = product(atom_normed, qkvg_ref[:, aw : 3 * aw]).astype(BF16)
    pick = (iota((LEFT_RIM, atoms), 1) == iota((LEFT_RIM, atoms), 0) + (count - LEFT_RIM))
    rims[0:LEFT_RIM, :] = product(pick.astype(F32).astype(BF16), keyval).astype(BF16)
    rims[LEFT_RIM:, :] = keyval[:RIGHT_RIM]

    pl.semaphore_wait(
        barrier,
        1 + (1 if ny > 1 else 0)
        + jnp.where(z + 1 < nz, 1, 0) + jnp.where(z > 0, 1, 0)
        + jnp.where(me + 1 < rows, 1, 0) + jnp.where(me > 0, 1, 0),
    )

    to_next = pltpu.make_async_remote_copy(
        rims.at[pl.ds(0, LEFT_RIM)], halo.at[pl.ds(0, LEFT_RIM)], halo_send.at[0], halo_recv.at[0],
        device_id={"row": me + 1}, device_id_type=MESH,
    )
    to_prior = pltpu.make_async_remote_copy(
        rims.at[pl.ds(LEFT_RIM, RIGHT_RIM)], halo.at[pl.ds(LEFT_RIM, RIGHT_RIM)],
        halo_send.at[1], halo_recv.at[1],
        device_id={"row": me - 1}, device_id_type=MESH,
    )
    pl.when(me + 1 < rows)(to_next.start)
    pl.when(me > 0)(to_prior.start)
    for load in loads[10:13]:
        load.start()

    queries = product(atom_normed, qkvg_ref[:, :aw]).astype(BF16)
    gates = jax.nn.sigmoid(product(atom_normed, qkvg_ref[:, 3 * aw :]).astype(BF16).astype(F32))
    blocks = atoms // WQ
    lane_head = iota((AH * WQ, aw), 1) // ahead
    own_head = (lane_head == iota((AH * WQ, aw), 0) // WQ).astype(F32)
    own_head_half = own_head.astype(BF16)
    span = atoms + RIGHT_RIM
    place = iota((span, WK), 0) - count
    chosen = ((place == iota((span, WK), 1) - LEFT_RIM) & (place >= 0)).astype(F32).astype(BF16)
    within = iota((span, 2 * aw), 0) - count
    within = (within >= 0) & (within < RIGHT_RIM)
    base_rows = jnp.concatenate(
        [keyval.astype(F32), jnp.zeros((RIGHT_RIM, 2 * aw), F32)], axis=0
    )
    ext[:, 2 * aw :] = jnp.ones((ext.shape[0], aw), BF16)
    load_abias.wait()
    load_token.wait()
    load_tgain.wait()
    load_aproj.wait()
    load_a2t.wait()
    load_tsingle.wait()
    pl.when(me > 0)(to_next.wait_recv)
    pl.when(me + 1 < rows)(to_prior.wait_recv)
    rim = halo[...]
    moved = product(chosen, rim)
    ext[0:LEFT_RIM, : 2 * aw] = rim[:LEFT_RIM]
    ext[LEFT_RIM:, : 2 * aw] = jnp.where(within, moved, base_rows).astype(BF16)

    is_first = me == 0
    is_last = me == rows - 1
    low = jnp.where(is_first, 0, -LEFT_RIM)
    high = jnp.where(is_last, count, atoms + WK)
    for start_at in range(0, blocks, 8):
        batch = range(start_at, min(start_at + 8, blocks))
        scores = []
        for w in batch:
            q = queries[w * WQ : (w + 1) * WQ]
            stacked = jnp.concatenate([q] * AH, axis=0) * own_head_half
            scores.append(product_t(stacked, ext[w * WQ : w * WQ + WK, :aw]))
        for at, w in enumerate(batch):
            value = scores[at] * ahead ** (-0.5) + abias[w].reshape(AH * WQ, WK).astype(F32)
            offset = iota((AH * WQ, WK), 1) + (WQ * w - LEFT_RIM)
            scores[at] = jnp.where((offset >= low) & (offset < high), value, MASKED)
        tops = [jnp.max(value, axis=-1, keepdims=True) for value in scores]
        raised = [jnp.exp(value - top) for value, top in zip(scores, tops)]
        results = [
            product(raised[at].astype(BF16), ext[w * WQ : w * WQ + WK, aw:])
            for at, w in enumerate(batch)
        ]
        for at, w in enumerate(batch):
            result = results[at][:, :aw] * own_head / results[at][:, aw:]
            att[w * WQ : (w + 1) * WQ, :] = jnp.sum(result.reshape(AH, WQ, aw), axis=0)
    gated = (att[...] * gates).astype(BF16)
    atom_mid = (x.astype(F32) + product(gated, aproj_ref[...])).astype(BF16)
    lifted = jnp.maximum(product(atom_mid, a2t[...]), 0.0).astype(BF16)
    member = (token_ref[...] == iota((toks, atoms), 0)) & (iota((toks, atoms), 1) < count)
    member_f = member.astype(F32)
    summed = product(member_f.astype(BF16), lifted)
    counts = jnp.sum(member_f, axis=1, keepdims=True)
    hidden = tsingle[...].astype(F32) + summed / counts
    normed = normalized(hidden, tgain_ref[...].reshape(1, tw))
    gathered[me] = normed

    piece_rows = toks // PIECES

    def copy(source, piece, way, target):
        view = gathered.at[source, pl.ds(piece * piece_rows, piece_rows)]
        return pltpu.make_async_remote_copy(
            view, view, send_sem.at[source, piece, way], recv_sem.at[source, piece],
            device_id={"row": target}, device_id_type=MESH,
        )

    def pass_up(source, piece, act):
        pl.when(z + 1 < nz)(lambda: act(copy(source, piece, 2, up)))

    def pass_down(source, piece, act):
        pl.when(z > 0)(lambda: act(copy(source, piece, 3, down)))

    def pass_near(source, piece, act):
        if ny > 1:
            act(copy(source, piece, 1, other))
        act(copy(source, piece, 0, sibling))

    start = lambda c: c.start()
    sent = lambda c: c.wait_send()

    def arrived(source, piece):
        copy(source, piece, 0, sibling).wait_recv()

    def own(act):
        for piece in range(PIECES):
            pass_up(me, piece, act)
            pass_down(me, piece, act)
            pass_near(me, piece, act)

    def along_z(distance, act, wait):
        for piece in range(PIECES):
            @pl.when(z - distance >= 0)
            def _():
                source = index(z - distance, y, core)
                if wait:
                    arrived(source, piece)
                pass_up(source, piece, act)
                pass_near(source, piece, act)

            @pl.when(z + distance < nz)
            def _():
                source = index(z + distance, y, core)
                if wait:
                    arrived(source, piece)
                pass_down(source, piece, act)
                pass_near(source, piece, act)

    def along_y(distance, act, wait):
        if ny == 1:
            return
        for piece in range(PIECES):
            for sign in (-1, 1):
                zz = z + sign * distance

                @pl.when((zz >= 0) & (zz < nz) & ((sign < 0) | (distance > 0)))
                def _():
                    source = index(zz, 1 - y, core)
                    if wait:
                        arrived(source, piece)
                    act(copy(source, piece, 0, sibling))

    own(start)
    turned = jnp.concatenate([member_f, member_f], axis=0).T.astype(BF16)

    for load in loads[13:]:
        load.start()
    load_tqg.wait()
    qgate = product(normed, tqg[...]).astype(BF16)
    turned_gate[...] = jax.nn.sigmoid(qgate[:, tw:].T.astype(F32))
    for group, (first, base) in enumerate(groups):
        part = qgate[:, base : base + 256].astype(F32)
        lanes = iota(part.shape, 1) + base
        spread_out = []
        for head in range(first, first + EACH):
            keep = (lanes >= head * thead) & (lanes < (head + 1) * thead)
            spread_out.append(jnp.where(keep, part, 0.0).astype(BF16))
        qbuf[group] = jnp.concatenate(spread_out, axis=0).T
    mbuf[...] = jnp.full(mbuf.shape, -jnp.inf, F32)
    lbuf[...] = jnp.zeros(lbuf.shape, F32)
    acc[...] = jnp.zeros(acc.shape, F32)
    load_tkv.wait()
    load_tbias.wait()

    def turn_bias(block, carry):
        keys = pl.ds(pl.multiple_of(block * 2 * toks, 2 * toks), 2 * toks)
        turned_bias[keys, :] = tbias[:, :, keys].reshape(TH * toks, 2 * toks).T
        return carry

    lax.fori_loop(0, rows // 2, turn_bias, 0)
    low_half = iota((thead, wide // 2), 1) < toks

    def attend(block):
        inputs = gathered[pl.ds(2 * block, 2)].reshape(2 * toks, tw)
        kv = product(inputs, tkv[...]).astype(BF16)
        turned_values = kv[:, tw:].T
        keys = pl.ds(pl.multiple_of(block * 2 * toks, 2 * toks), 2 * toks)
        scores = jnp.concatenate(
            [product(kv[:, base : base + 256], qbuf[group]) for group, (first, base) in enumerate(groups)], axis=1
        )
        scores = scores * thead ** (-0.5) + turned_bias[keys, :].astype(F32)
        old = mbuf[...]
        new = jnp.maximum(old, jnp.max(scores, axis=0, keepdims=True))
        factor = jnp.exp(old - new)
        raised = jnp.exp(scores - new)
        mbuf[...] = new
        lbuf[...] = lbuf[...] * factor + jnp.sum(raised, axis=0, keepdims=True)
        weights = raised.astype(BF16)
        updates = [
            product(turned_values[first * thead : (first + EACH) * thead], weights[:, group * wide : (group + 1) * wide])
            for group, (first, base) in enumerate(groups)
        ]
        both = []
        for update in updates:
            for half in range(EACH // 2):
                lanes = slice(half * 2 * toks, (half + 1) * 2 * toks)
                top = 2 * half * thead
                both.append(jnp.where(low_half, update[top : top + thead, lanes], update[top + thead : top + 2 * thead, lanes]))
        acc[...] = acc[...] * factor + jnp.concatenate(both, axis=1)

    def step(t, carry):
        distance = t // (2 * ny)
        turn = t % (2 * ny)

        @pl.when(turn == 0)
        def _():
            along_z(distance + 1, start, True)

        @pl.when(turn == 1)
        def _():
            along_y(distance, start, True)

        yy = jnp.where(turn // 2 == 0, y, 1 - y)
        sign = turn % 2
        zz = z + (2 * sign - 1) * distance

        @pl.when((zz >= 0) & (zz < nz) & ((sign == 0) | (distance > 0)))
        def _():
            for piece in range(PIECES):
                arrived(index(zz, yy, 1 - core), piece)
            attend(zz * ny + yy)

        return carry

    lax.fori_loop(0, nz * 2 * ny, step, 0)

    whole = acc[...] / lbuf[...]
    columns = [whole[:, head * toks : (head + 1) * toks] for head in range(TH)]
    attended = jnp.concatenate(columns, axis=0)
    tok_gated = (attended * turned_gate[...]).astype(BF16).T
    load_tproj.wait()
    token_out = (hidden + product(tok_gated, tproj[...])).astype(BF16)
    tout_ref[...] = token_out
    load_t2a.wait()
    back = product(token_out, t2a[...])
    high_part = back.astype(BF16)
    rest = back - high_part.astype(F32)
    spread = product(turned, jnp.concatenate([high_part, rest.astype(BF16)], axis=0))
    live = iota((atoms, aw), 0) < count
    aout_ref[...] = jnp.where(live, atom_mid.astype(F32) + spread, 0.0).astype(BF16)

    pl.when(me + 1 < rows)(to_next.wait_send)
    pl.when(me > 0)(to_prior.wait_send)
    own(sent)

    def drain(distance, carry):
        along_z(distance, sent, False)
        along_y(distance - 1, sent, False)
        return carry

    lax.fori_loop(1, nz, drain, 0)
    along_y(nz - 1, sent, False)


def hand_on(a_ref, t_ref, aout_ref, tout_ref, sem):
    copies = [
        pltpu.make_async_copy(a_ref, aout_ref, sem.at[0]),
        pltpu.make_async_copy(t_ref, tout_ref, sem.at[1]),
    ]
    for copy in copies:
        copy.start()
    for copy in copies:
        copy.wait()


def on_device(
    rows, ny, atom_single, atom_count, atom_token, atom_bias, token_single, token_bias,
    atom_gain, atom_qkvg, atom_proj, atom_to_token, token_gain, token_qg, token_kv,
    token_proj, token_to_atom,
):
    atoms, aw = atom_single.shape
    toks, tw = token_single.shape
    vmem = pl.BlockSpec(memory_space=pltpu.VMEM)
    anywhere = pl.BlockSpec(memory_space=pl.ANY)
    taken = [
        atom_single, atom_gain.reshape(1, aw), atom_qkvg, atom_bias, atom_token.reshape(1, atoms), token_gain,
        atom_proj, atom_to_token, token_single, token_qg, token_kv, token_bias, token_proj, token_to_atom,
    ]
    results = pl.pallas_call(
        functools.partial(kernel, rows, ny),
        out_shape=(pltpu.VMEM((atoms, aw), BF16), pltpu.VMEM((toks, tw), BF16)),
        in_specs=[anywhere] * (1 + len(taken)),
        out_specs=(vmem, vmem),
        scratch_shapes=[pltpu.SMEM(atom_count.shape, atom_count.dtype)]
        + [pltpu.VMEM(a.shape, a.dtype) for a in taken]
        + [
            pltpu.VMEM((LEFT_RIM + RIGHT_RIM, 2 * aw), BF16),
            pltpu.VMEM((LEFT_RIM + RIGHT_RIM, 2 * aw), BF16),
            pltpu.VMEM((LEFT_RIM + atoms + RIGHT_RIM, 3 * aw), BF16),
            pltpu.VMEM((atoms, aw), F32),
            pltpu.VMEM((rows, toks, tw), BF16),
            pltpu.VMEM((TH // EACH, 256, EACH * toks), BF16),
            pltpu.VMEM((rows * toks, TH * toks), BF16),
            pltpu.VMEM((tw, toks), F32),
            pltpu.VMEM((1, TH * toks), F32),
            pltpu.VMEM((1, TH * toks), F32),
            pltpu.VMEM((tw // TH, TH * toks), F32),
            pltpu.SemaphoreType.DMA((1 + len(taken),)),
            pltpu.SemaphoreType.DMA((2,)),
            pltpu.SemaphoreType.DMA((2,)),
            pltpu.SemaphoreType.DMA((rows, PIECES, 4)),
            pltpu.SemaphoreType.DMA((rows, PIECES)),
        ],
        compiler_params=pltpu.CompilerParams(collective_id=0, has_side_effects=True),
    )(atom_count, *taken)
    held = [pltpu.with_memory_space_constraint(r, pltpu.VMEM) for r in results]
    return pl.pallas_call(
        hand_on,
        out_shape=tuple(jax.ShapeDtypeStruct(r.shape, r.dtype) for r in results),
        in_specs=(vmem, vmem),
        out_specs=(anywhere, anywhere),
        scratch_shapes=[pltpu.SemaphoreType.DMA((2,))],
    )(*held)


def chips_across(mesh):
    rows = mesh.shape["row"]
    group = mesh.devices.reshape(-1)[:rows]
    places = [getattr(device, "coords", None) for device in group]
    if any(place is None for place in places):
        return 1
    wide = len({place[1] for place in places})
    return 2 if wide == 2 and rows % 4 == 0 else 1


def solution(mesh):
    rows = mesh.shape["row"]
    return jax.shard_map(
        functools.partial(on_device, rows, chips_across(mesh)),
        mesh=mesh,
        in_specs=(
            P(("sample", "row"), None),
            P(),
            P("row"),
            P("row", None, None, None),
            P(("sample", "row"), None),
            P(None, "row", None),
            P(), P(), P(), P(), P(), P(), P(), P(), P(),
        ),
        out_specs=(P(("sample", "row"), None), P(("sample", "row"), None)),
        check_vma=False,
    )
```
